128 devices in a mesh: dp: 4 (over y), fsdp: 4 (over x_lo, core), ctx: 8 (over z, x_hi).
Axes of the slice: x: 4 (x_hi: 2, x_lo: 2; x = x_hi * 2 + x_lo), y: 4, z: 4, core: 2. Of those that a mesh axis runs over, the one named last changes fastest.
Arguments:
- tokens: bfloat16 [16, 4096, 1024], P(('dp', 'fsdp'), 'ctx')
- bounds: int32 [16, 4096], P(('dp', 'fsdp'), 'ctx'), may hold values 0 or 1
- decay_rates: float32 [16], replicated, may hold values from 2.4414063e-05 to 0.9
- w_query: bfloat16 [1024, 1024], P('fsdp')
- w_key: bfloat16 [1024, 1024], P('fsdp')
- w_up: bfloat16 [1024, 2048], P('fsdp'), may hold values from -0.1875 to 0.1875
- grad_out: bfloat16 [16, 4096, 2048], P(('dp', 'fsdp'), 'ctx'), may hold values from -6 to 6
Outputs:
- dechunked: bfloat16 [16, 4096, 2048], P(('dp', 'fsdp'), 'ctx')
- grad_tokens: bfloat16 [16, 4096, 1024], P(('dp', 'fsdp'), 'ctx')
- grad_query: float32 [1024, 1024], P('fsdp')
- grad_key: float32 [1024, 1024], P('fsdp')
- grad_up: float32 [1024, 2048], P('fsdp')
The draws below stay inside these ranges and needn't reach their ends.
All inputs are finite; a program needn't handle non-finite values. No bound on the sum of `bounds` on one device may be relied on, other than what follows from the above.
Results may differ from the reference program's by a relative error of at most 0.0049.
Values may be sent and summed in bfloat16 or wider, within the bound.
No kernel may reach another device: no remote copies, remote signals or barrier semaphores. Data moves between devices by JAX's collectives and lax.ppermute only.
A program may use at most 128 MiB of HBM per device.

```python
import math
import jax
import jax.numpy as jnp
from jax import lax

D = 1024
E = 2048
HEADS = 16
SEQ = 4096
BATCH = 16


def draw_tokens(key, part):
    base = jax.random.fold_in(key, 11)
    first_key, second_key, third_key = jax.random.split(base, 3)
    noise = jax.random.normal(first_key, (BATCH, SEQ + 1, D), jnp.float32)
    own_part = jax.random.uniform(second_key, (BATCH, SEQ, 1), jnp.float32, 0.5, 1.0)
    shared_part = jax.random.uniform(third_key, (BATCH, SEQ, 1), jnp.float32, -1.0, 1.0)
    return (own_part * noise[:, 1:] + shared_part * noise[:, :-1]).astype(jnp.bfloat16)


def near_identity(key):
    noise = jax.random.normal(key, (D, D), jnp.float32)
    return (jnp.eye(D, dtype=jnp.float32) + noise * (0.5 / D ** 0.5)).astype(jnp.bfloat16)


def draw_w_query(key, part):
    return near_identity(jax.random.fold_in(key, 21))


def draw_w_key(key, part):
    return near_identity(jax.random.fold_in(key, 22))


def touch_ends(result, rng, smallest, top_value):
    extent = result.shape
    spot = [jax.random.randint(jax.random.fold_in(rng, axis), (), 0, extent[axis]) for axis in range(len(extent))]
    result = result.at[tuple(spot)].set(smallest)
    longest = extent.index(max(extent))
    spot[longest] = (spot[longest] + 1) % extent[longest]
    return result.at[tuple(spot)].set(top_value)


def steps_of(rng, extent, cuts, low, high):
    level = 1.0
    for position, parts in cuts:
        steps = jax.random.uniform(jax.random.fold_in(jax.random.fold_in(rng, 6), position), (parts,), jnp.float32, low / len(cuts), high / len(cuts))
        level = level * jnp.repeat(jnp.exp(steps), extent[position] // parts).reshape((-1,) + (1,) * (len(extent) - 1 - position))
    return level


def bell_draw(key, extent, spread, most, shards=(), kind=jnp.bfloat16):
    array = spread * jax.random.normal(key, extent, jnp.float32)
    if shards:
        array = array * steps_of(key, extent, shards, -0.22, 0.18)
    return jnp.clip(array, -most, most).astype(kind)


def setup_inputs(seed: int = 0) -> dict:
    key_list = jax.random.split(jax.random.key(seed), 8)
    return {
        "tokens": draw_tokens(jax.random.fold_in(key_list[7], 71), 0),
        "bounds": touch_ends((jax.random.randint(key_list[1], (BATCH, SEQ), 0, 6) < 1).astype(jnp.int32), jax.random.fold_in(key_list[1], 1), 0, 1),
        "decay_rates": jnp.clip(jnp.exp(jax.random.uniform(key_list[2], (HEADS,), jnp.float32, math.log(2.441406286379788e-05), math.log(0.9))), 2.441406286379788e-05, 0.9),
        "w_query": draw_w_query(jax.random.fold_in(key_list[7], 71), 0),
        "w_key": draw_w_key(jax.random.fold_in(key_list[7], 71), 0),
        "w_up": bell_draw(key_list[5], (D, E), D ** -0.5, 0.1875, ((0, 4),)),
        "grad_out": bell_draw(key_list[6], (BATCH, SEQ, E), 1.0, 6.0, ((0, 16), (1, 8))),
    }


epsilon = 1e-06

def one_sequence(tokens_row, bounds_row, grad_row, w_query, w_key, w_up, decay_rates):
    length = tokens_row.shape[0]
    model_width = w_query.shape[0]
    head_count = decay_rates.shape[0]
    queries = jnp.dot(tokens_row, w_query, preferred_element_type=jnp.float32)
    keys_now = jnp.dot(tokens_row, w_key, preferred_element_type=jnp.float32)
    values = jnp.dot(tokens_row, w_up, preferred_element_type=jnp.float32)
    keys_prev = jnp.concatenate([jnp.zeros((1, model_width), jnp.float32), keys_now[:-1]], 0)
    inv_query = lax.rsqrt(lax.optimization_barrier(jnp.sum(queries * queries, -1)) + epsilon)
    inv_key = lax.rsqrt(lax.optimization_barrier(jnp.sum(keys_prev * keys_prev, -1)) + epsilon)
    cosine = lax.optimization_barrier(jnp.sum(queries * keys_prev, -1)) * inv_query * inv_key
    opening = jnp.arange(length) == 0
    boundary_prob = jnp.where(opening, 1.0, 0.5 * (1.0 - cosine))
    marked = jnp.where(opening, 1.0, bounds_row.astype(jnp.float32))
    mix_rate = (marked * boundary_prob)[:, None] * decay_rates[None, :]
    value_groups = values.reshape(length, head_count, -1)

    def forward_step(carried, element):
        rate_now, value_now = element
        carried = rate_now[:, None] * value_now + (1.0 - rate_now[:, None]) * carried
        return (carried, carried)
    zero_state = jnp.zeros(value_groups.shape[1:], jnp.float32)
    _, states = lax.scan(forward_step, zero_state, (mix_rate, value_groups))
    states_prev = jnp.concatenate([zero_state[None], states[:-1]], 0)
    cotangent = grad_row.astype(jnp.float32).reshape(length, head_count, -1)

    def backward_step(carried, element):
        rate_now, incoming = element
        adjoint = incoming + carried
        return ((1.0 - rate_now[:, None]) * adjoint, adjoint)
    _, adjoints = lax.scan(backward_step, zero_state, (mix_rate, cotangent), reverse=True)
    d_values = (mix_rate[:, :, None] * adjoints).reshape(length, -1).astype(jnp.bfloat16)
    d_rate = lax.optimization_barrier(jnp.sum(adjoints * (value_groups - states_prev), -1))
    d_prob = jnp.where(opening, 0.0, marked * lax.optimization_barrier(jnp.sum(d_rate * decay_rates[None, :], -1)))
    d_cos = -0.5 * d_prob
    pair_scale = inv_query * inv_key
    d_query = (d_cos[:, None] * (keys_prev * pair_scale[:, None] - (cosine * inv_query * inv_query)[:, None] * queries)).astype(jnp.bfloat16)
    d_prev = d_cos[:, None] * (queries * pair_scale[:, None] - (cosine * inv_key * inv_key)[:, None] * keys_prev)
    d_key = jnp.concatenate([d_prev[1:], jnp.zeros((1, model_width), jnp.float32)], 0).astype(jnp.bfloat16)
    d_all = jnp.concatenate([d_query, d_key, d_values], 1)
    panels = jnp.concatenate([w_query, w_key, w_up], 1)
    d_tokens = lax.dot_general(d_all, panels, (((1,), (1,)), ((), ())), preferred_element_type=jnp.float32).astype(jnp.bfloat16)
    grads = lax.dot_general(tokens_row, d_all, (((0,), (0,)), ((), ())), preferred_element_type=jnp.float32)
    return (states.reshape(length, -1).astype(jnp.bfloat16), d_tokens, grads)

def reference(tokens, bounds, decay_rates, w_query, w_key, w_up, grad_out):
    model_width = w_query.shape[0]

    def sequence_step(grad_sum, element):
        tokens_row, bounds_row, grad_row = element
        dechunked_row, d_tokens, grads = one_sequence(tokens_row, bounds_row, grad_row, w_query, w_key, w_up, decay_rates)
        return (grad_sum + grads, (dechunked_row, d_tokens))
    initial = jnp.zeros((model_width, 2 * model_width + w_up.shape[1]), jnp.float32)
    grad_sum, (dechunked, grad_tokens) = lax.scan(sequence_step, initial, (tokens, bounds, grad_out))
    return (dechunked, grad_tokens, grad_sum[:, :model_width], grad_sum[:, model_width:2 * model_width], grad_sum[:, 2 * model_width:])
```

```python
import jax
import jax.numpy as jnp
from jax import lax
from jax.sharding import PartitionSpec as P

SPAN = 128
epsilon = 1e-06
CTX = ("z", "xh")


def along_x(a, by):
    pairs = []
    for xl in range(2):
        for xh in range(2):
            x = (xh * 2 + xl + by) % 4
            pairs.append((xl * 2 + xh, (x % 2) * 2 + x // 2))
    return lax.ppermute(a, ("xl", "xh"), pairs)


def swap_core(a):
    return lax.ppermute(a, "core", [(0, 1), (1, 0)])


def along_ctx(a, by):
    return lax.ppermute(a, CTX, [(i, i + by) for i in range(8) if 0 <= i + by < 8])


def gather_pieces(w):
    half = w.shape[0] // 2
    low, high = along_x(w[:half], -1), along_x(w[half:], 1)
    near = swap_core(w)
    far = jnp.concatenate([low, high], 0)
    return [w, near, far, swap_core(far)]


def spread(a, axes, count):
    return lax.all_to_all(jnp.broadcast_to(a[None], (count,) + a.shape), axes, 0, 0, tiled=True)


def per_device(tokens, bounds, decay_rates, w_query, w_key, w_up, grad_out):
    _, length, width = tokens.shape
    hidden = w_up.shape[1]
    heads = decay_rates.shape[0]
    channels = hidden // heads
    blocks = length // SPAN
    tok = tokens[0]
    own_ctx = lax.axis_index(CTX)
    core = lax.axis_index("core")
    shard = lax.axis_index("xl") * 2 + core

    before = along_ctx(tok[-1:], 1)
    tok_prev = jnp.concatenate([before, tok[:-1]], 0)
    panels = jnp.concatenate([w_query, w_key, w_up], 1)
    rows = panels.shape[0]
    full = jnp.zeros((4 * rows, panels.shape[1]), panels.dtype)
    for j, piece in enumerate(gather_pieces(panels)):
        full = lax.dynamic_update_slice(full, piece, ((shard ^ j) * rows, 0))
    wq, wk, wu = full[:, :width], full[:, width : 2 * width], full[:, 2 * width :]
    queries = jnp.dot(tok, wq, preferred_element_type=jnp.float32)
    keys_prev = jnp.dot(tok_prev, wk, preferred_element_type=jnp.float32)
    values = jnp.dot(tok, wu, preferred_element_type=jnp.float32)

    inv_query = lax.rsqrt(jnp.sum(queries * queries, -1) + epsilon)
    inv_key = lax.rsqrt(jnp.sum(keys_prev * keys_prev, -1) + epsilon)
    cosine = jnp.sum(queries * keys_prev, -1) * inv_query * inv_key
    opening = jnp.logical_and(own_ctx == 0, jnp.arange(length) == 0)
    prob = jnp.where(opening, 1.0, 0.5 * (1.0 - cosine))
    marked = jnp.where(opening, 1.0, bounds[0].astype(jnp.float32))
    mix_rate = (marked * prob)[:, None] * decay_rates
    rate_blocks = mix_rate.reshape(blocks, SPAN, heads)
    log_keep = jnp.cumsum(jnp.log(1.0 - rate_blocks), axis=1)
    keep_heads = jnp.moveaxis(log_keep, 2, 1)
    log_gap = keep_heads[..., :, None] - keep_heads[..., None, :]
    offsets = jnp.arange(SPAN)
    lower = offsets[:, None] >= offsets[None, :]
    band = jnp.where(lower, jnp.exp(jnp.where(lower, log_gap, -1e30)), 0.0)
    value_blocks = values.reshape(blocks, SPAN, heads, channels)
    cotangent = grad_out[0].astype(jnp.float32).reshape(blocks, SPAN, heads, channels)
    local_states = jnp.einsum(
        "nhtu,nuhc->nthc", band, value_blocks * rate_blocks[..., None],
        precision=lax.Precision.HIGHEST,
    )
    local_adjoint = jnp.einsum(
        "nhut,nuhc->nthc", band, cotangent, precision=lax.Precision.HIGHEST
    )
    block_logs = log_keep[:, -1]
    block_decay = jnp.exp(block_logs)
    zero = jnp.zeros((heads, channels), jnp.float32)
    block_in, state = [], zero
    for n in range(blocks):
        block_in.append(state)
        state = block_decay[n][:, None] * state + local_states[n, -1]
    heads_first = (1.0 - rate_blocks[:, 0])[..., None] * local_adjoint[:, 0]
    block_out, head = [None] * blocks, zero
    for n in reversed(range(blocks)):
        block_out[n] = head
        head = block_decay[n][:, None] * head + heads_first[n]
    running = jnp.cumsum(block_logs, axis=0)
    decay_before = jnp.exp(running - block_logs)
    decay_after = jnp.exp(running[-1:] - running)
    decay = jnp.broadcast_to(jnp.exp(running[-1])[:, None], (heads, channels))
    parts = spread(jnp.concatenate([state, head, decay], 1), CTX, 8)
    state_in, adjoint_in = zero, zero
    for j in range(8):
        s, d = parts[j, :, :channels], parts[j, :, 2 * channels :]
        state_in = jnp.where(j < own_ctx, d * state_in + s, state_in)
    for j in reversed(range(8)):
        a, d = parts[j, :, channels : 2 * channels], parts[j, :, 2 * channels :]
        adjoint_in = jnp.where(j > own_ctx, d * adjoint_in + a, adjoint_in)
    carry = jnp.stack(block_in) + decay_before[..., None] * state_in
    states = local_states + jnp.exp(log_keep)[..., None] * carry[:, None]
    back = jnp.stack(block_out) + decay_after[..., None] * adjoint_in
    adjoints = local_adjoint + jnp.exp(log_keep[:, -1:] - log_keep)[..., None] * back[:, None]
    state_rows = states.reshape(length, heads, channels)
    adjoint_rows = adjoints.reshape(length, heads, channels)
    states_prev = jnp.concatenate([state_in[None], state_rows[:-1]], 0)
    dechunked = state_rows.reshape(1, length, hidden).astype(jnp.bfloat16)
    d_values = (mix_rate[..., None] * adjoint_rows).reshape(length, hidden).astype(jnp.bfloat16)
    d_rate = jnp.sum(adjoint_rows * (values.reshape(length, heads, channels) - states_prev), -1)
    d_prob = jnp.where(opening, 0.0, marked * jnp.sum(d_rate * decay_rates, -1))
    d_cos = -0.5 * d_prob
    pair = inv_query * inv_key
    d_query = (
        d_cos[:, None]
        * (keys_prev * pair[:, None] - (cosine * inv_query * inv_query)[:, None] * queries)
    ).astype(jnp.bfloat16)
    d_prev = (
        d_cos[:, None]
        * (queries * pair[:, None] - (cosine * inv_key * inv_key)[:, None] * keys_prev)
    ).astype(jnp.bfloat16)

    def share(which):
        cols = lambda t: jnp.concatenate(
            [lax.dynamic_slice_in_dim(t, (2 * b + which) * rows, rows, 1) for b in range(2)], 1
        )
        dims = (((0,), (0,)), ((), ()))
        now, prev = cols(tok), cols(tok_prev)
        parts = [
            lax.dot_general(t, d, dims, preferred_element_type=jnp.float32)
            for t, d in ((now, d_query), (prev, d_prev), (now, d_values))
        ]
        return jnp.concatenate(parts, 1)

    theirs = swap_core(share(1 - core).astype(jnp.bfloat16))
    pair_sum = share(core) + theirs.astype(jnp.float32)
    ranks = 2 * 32
    exchanged = lax.all_to_all(
        pair_sum.astype(jnp.bfloat16).reshape(ranks, -1, pair_sum.shape[1]),
        ("xl", "dp", "z", "xh"), 0, 0, tiled=True,
    )
    total = jnp.sum(exchanged.astype(jnp.float32), 0).astype(jnp.bfloat16)
    summed = spread(total, ("dp", "z", "xh"), 32).reshape(rows, -1).astype(jnp.float32)

    dims = (((1,), (1,)), ((), ()))
    d_next = lax.dot_general(d_prev, wk, dims, preferred_element_type=jnp.float32)
    after = along_ctx(d_next[:1], -1)
    d_tokens = lax.dot_general(
        jnp.concatenate([d_query, d_values], 1), jnp.concatenate([wq, wu], 1), dims,
        preferred_element_type=jnp.float32,
    ) + jnp.concatenate([d_next[1:], after], 0)
    return (
        dechunked,
        d_tokens.astype(jnp.bfloat16)[None],
        summed[:, :width],
        summed[:, width : 2 * width],
        summed[:, 2 * width :],
    )


def solution(mesh):
    split = jax.sharding.Mesh(
        mesh.devices.reshape(4, 2, 2, 4, 2), ("dp", "xl", "core", "z", "xh")
    )
    rows = P(("xl", "core"), None)
    data = P(("dp", "xl", "core"), CTX, None)
    return jax.shard_map(
        per_device,
        mesh=split,
        in_specs=(data, P(("dp", "xl", "core"), CTX), P(), rows, rows, rows, data),
        out_specs=(data, data, rows, rows, rows),
        check_vma=False,
    )
```

```python
import functools

import jax
import jax.numpy as jnp
from jax import lax
from jax.experimental import pallas as pl
from jax.experimental.pallas import tpu as pltpu
from jax.sharding import PartitionSpec as P

SPAN = 128
LANES = 128
epsilon = 1e-06
CTX = ("z", "xh")
RANGES = 8
HIGHEST = lax.Precision.HIGHEST
F32 = jnp.float32
BF16 = jnp.bfloat16


def along_x(a, by):
    pairs = []
    for xl in range(2):
        for xh in range(2):
            x = (xh * 2 + xl + by) % 4
            pairs.append((xl * 2 + xh, (x % 2) * 2 + x // 2))
    return lax.ppermute(a, ("xl", "xh"), pairs)


def swap_core(a):
    return lax.ppermute(a, "core", [(0, 1), (1, 0)])


def along_ctx(a, by):
    return lax.ppermute(
        a, CTX, [(i, i + by) for i in range(RANGES) if 0 <= i + by < RANGES]
    )


def spread(a, axes, count):
    return lax.all_to_all(jnp.broadcast_to(a[None], (count,) + a.shape), axes, 0, 0, tiled=True)


def mxu(a, b):
    return jnp.dot(a, b, preferred_element_type=F32)


def halves(a):
    high = a.astype(BF16)
    return high, (a - high.astype(F32)).astype(BF16)


def ids(shape, dim):
    return lax.broadcasted_iota(jnp.int32, shape, dim)


def assemble(place, pieces, whole):
    rows = pieces[0].shape[0]
    shard = place[0]
    for j, piece in enumerate(pieces):
        start = pl.multiple_of((shard ^ j) * rows, rows)
        whole[pl.ds(start, rows), :] = piece[...]


def head_cols(h):
    return slice(h * LANES, (h + 1) * LANES)


def rates_kernel(
    place, tok, tok_prev, bounds, decay, cot, q0, q1, q2, q3, k0, k1, k2, k3,
    queries, keys, mix_out, keep_out, stats_out, adjoint, outs, message,
    wq, wk, carry,
):
    heads = adjoint.shape[1] // LANES
    blocks = adjoint.shape[0] // SPAN
    assemble(place, (q0, q1, q2, q3), wq)
    assemble(place, (k0, k1, k2, k3), wk)
    queries[...] = mxu(tok[...], wq[...])
    keys[...] = mxu(tok_prev[...], wk[...])
    carry[...] = jnp.zeros_like(carry)
    carry[1:2, :] = jnp.ones((1, carry.shape[1]), F32)

    @pl.loop(0, blocks)
    def _(step):
        n = blocks - 1 - step
        rows = pl.ds(pl.multiple_of(n * SPAN, SPAN), SPAN)
        q, k = queries[rows, :], keys[rows, :]
        iq = lax.rsqrt(jnp.sum(q * q, -1, keepdims=True) + epsilon)
        ik = lax.rsqrt(jnp.sum(k * k, -1, keepdims=True) + epsilon)
        cosine = jnp.sum(q * k, -1, keepdims=True) * iq * ik
        lane = ids((SPAN, LANES), 1)
        sub = ids((SPAN, LANES), 0)
        first = jnp.logical_and(place[1] == 0, n == 0)
        opening = jnp.logical_and(first, ids((SPAN, 1), 0) == 0)
        prob = jnp.where(opening, 1.0, 0.5 * (1.0 - cosine))
        marked = jnp.where(opening, 1.0, bounds[rows, :])
        mix = (marked * prob) * decay[...]
        logs = jnp.log(1.0 - mix)
        lower = (sub >= lane).astype(F32)
        keep = jnp.dot(lower, logs, precision=HIGHEST, preferred_element_type=F32)
        keep_rows = keep.T
        active = jnp.where(opening, 0.0, marked)
        stats = jnp.where(lane == 0, iq, jnp.where(lane == 1, ik, jnp.where(lane == 2, cosine, active)))
        mix_out[rows, :] = mix
        keep_out[rows, :] = keep
        stats_out[rows, :] = stats
        outs[pl.ds(n, 1), :] = carry[0:1, :]
        total = jnp.exp(keep[SPAN - 1 : SPAN, :])
        upper = sub <= lane
        for h in range(heads):
            cols = head_cols(h)
            gap = keep_rows[h : h + 1, :] - keep[:, h : h + 1]
            band = jnp.where(upper, jnp.exp(jnp.where(upper, gap, 0.0)), 0.0)
            high, low = halves(band)
            g = cot[rows, cols]
            local = mxu(high, g) + mxu(low, g)
            adjoint[rows, cols] = local
            d = total[:, h : h + 1]
            carry[0:1, cols] = d * carry[0:1, cols] + (1.0 - mix[0:1, h : h + 1]) * local[0:1, :]
            carry[1:2, cols] = d * carry[1:2, cols]

    for j in range(RANGES):
        message[j] = carry[...]


def states_kernel(
    place, tok, mix_ref, keep_ref, u0, u1, u2, u3,
    values, states, ins, message, wu, carry,
):
    heads = values.shape[1] // LANES
    blocks = values.shape[0] // SPAN
    assemble(place, (u0, u1, u2, u3), wu)
    values[...] = mxu(tok[...], wu[...])
    carry[...] = jnp.zeros_like(carry)

    @pl.loop(0, blocks)
    def _(n):
        rows = pl.ds(pl.multiple_of(n * SPAN, SPAN), SPAN)
        mix, keep = mix_ref[rows, :], keep_ref[rows, :]
        keep_rows = keep.T
        lower = ids((SPAN, LANES), 0) >= ids((SPAN, LANES), 1)
        ins[pl.ds(n, 1), :] = carry[0:1, :]
        total = jnp.exp(keep[SPAN - 1 : SPAN, :])
        for h in range(heads):
            cols = head_cols(h)
            gap = keep[:, h : h + 1] - keep_rows[h : h + 1, :]
            band = jnp.where(lower, jnp.exp(jnp.where(lower, gap, 0.0)), 0.0)
            high, low = halves(band)
            added, rest = halves(mix[:, h : h + 1] * values[rows, cols])
            local = mxu(high, added) + mxu(low, added) + mxu(high, rest)
            states[rows, cols] = local
            carry[0:1, cols] = total[:, h : h + 1] * carry[0:1, cols] + local[SPAN - 1 : SPAN, :]

    for j in range(RANGES):
        message[j] = carry[...]


def adjoint_kernel(place, local, outs, mix_ref, keep_ref, messages, adjoint, d_values):
    heads = adjoint.shape[1] // LANES
    blocks = adjoint.shape[0] // SPAN
    own = place[1]
    incoming = jnp.zeros((1, adjoint.shape[1]), F32)
    for j in reversed(range(RANGES)):
        nearer = messages[j, 1:2, :] * incoming + messages[j, 0:1, :]
        incoming = jnp.where(j > own, nearer, incoming)

    def block(step, after):
        n = blocks - 1 - step
        rows = pl.ds(pl.multiple_of(n * SPAN, SPAN), SPAN)
        mix, keep = mix_ref[rows, :], keep_ref[rows, :]
        last = keep[SPAN - 1 : SPAN, :]
        fade = jnp.exp(last - keep)
        spread_after = jnp.exp(after)
        back = outs[pl.ds(n, 1), :]
        for h in range(heads):
            cols = head_cols(h)
            tail = back[:, cols] + spread_after[:, h : h + 1] * incoming[:, cols]
            full = local[rows, cols] + fade[:, h : h + 1] * tail
            adjoint[rows, cols] = full
            d_values[rows, cols] = (mix[:, h : h + 1] * full).astype(BF16)
        return after + last

    lax.fori_loop(0, blocks, block, jnp.zeros((1, LANES), F32))


def router_kernel(
    place, local, ins, keep_ref, stats_ref, decay, messages, decays, values, adjoint, queries, keys,
    dechunked, d_query, d_prev,
):
    heads = values.shape[1] // LANES
    blocks = values.shape[0] // SPAN
    own = place[1]
    incoming = jnp.zeros((1, values.shape[1]), F32)
    for j in range(RANGES):
        nearer = decays[j, 1:2, :] * incoming + messages[j, 0:1, :]
        incoming = jnp.where(j < own, nearer, incoming)

    def block(n, before):
        rows = pl.ds(pl.multiple_of(n * SPAN, SPAN), SPAN)
        keep = keep_ref[rows, :]
        fade = jnp.exp(keep)
        reach = jnp.exp(before)
        start = ins[pl.ds(n, 1), :]
        top = ids((SPAN, LANES), 0) == 0
        total = jnp.zeros((SPAN, LANES), F32)
        for h in range(heads):
            cols = head_cols(h)
            base = start[:, cols] + reach[:, h : h + 1] * incoming[:, cols]
            state = local[rows, cols] + fade[:, h : h + 1] * base
            dechunked[rows, cols] = state.astype(BF16)
            earlier = jnp.where(top, base, pltpu.roll(state, 1, 0))
            moved = adjoint[rows, cols] * (values[rows, cols] - earlier)
            total = total + decay[:, h : h + 1] * moved
        stats = stats_ref[rows, :]
        iq, ik, cosine, active = (stats[:, i : i + 1] for i in range(4))
        d_cos = -0.5 * (active * jnp.sum(total, -1, keepdims=True))
        both = d_cos * (iq * ik)
        over_q, over_k = d_cos * (cosine * iq * iq), d_cos * (cosine * ik * ik)
        q, k = queries[rows, :], keys[rows, :]
        d_query[rows, :] = (k * both - over_q * q).astype(BF16)
        d_prev[rows, :] = (q * both - over_k * k).astype(BF16)
        return before + keep[SPAN - 1 : SPAN, :]

    lax.fori_loop(0, blocks, block, jnp.zeros((1, LANES), F32))


def tokens_kernel(place, d_query, d_key, d_values, *refs):
    out = refs[-1]
    dims = (((1,), (1,)), ((), ()))
    for j in range(4):
        wq, wk, wu = refs[3 * j : 3 * j + 3]
        rows = wq.shape[0]
        start = pl.multiple_of((place[0] ^ j) * rows, rows)
        terms = [
            lax.dot_general(d[...], w[...], dims, preferred_element_type=F32)
            for d, w in ((d_query, wq), (d_key, wk), (d_values, wu))
        ]
        out[:, pl.ds(start, rows)] = (terms[0] + terms[1] + terms[2]).astype(BF16)


def call(body, outs, scratch, flops, *args):
    smem = pl.BlockSpec(memory_space=pltpu.SMEM)
    vmem = pl.BlockSpec(memory_space=pltpu.VMEM)
    return pl.pallas_call(
        body,
        out_shape=[jax.ShapeDtypeStruct(s, t) for s, t in outs],
        in_specs=[smem] + [vmem] * (len(args) - 1),
        out_specs=[vmem] * len(outs),
        scratch_shapes=scratch,
        cost_estimate=pl.CostEstimate(flops=flops, bytes_accessed=0, transcendentals=0),
        compiler_params=pltpu.CompilerParams(vmem_limit_bytes=VMEM_LIMIT),
    )(*args)


VMEM_LIMIT = 24 * 1024 * 1024


def per_device(tokens, bounds, decay_rates, w_query, w_key, w_up, grad_out):
    _, length, width = tokens.shape
    hidden = w_up.shape[1]
    heads = decay_rates.shape[0]
    rows = w_query.shape[0]
    blocks = length // SPAN
    tok, cot = tokens[0], grad_out[0]
    core = lax.axis_index("core")
    place = jnp.stack([lax.axis_index("xl") * 2 + core, lax.axis_index(CTX)]).astype(jnp.int32)

    q2, k2 = along_x(w_query, -1), along_x(w_key, 1)
    half = rows // 2
    low, high = along_x(w_up[:half], -1), along_x(w_up[half:], 1)
    q1, k1 = swap_core(w_query), swap_core(w_key)
    before = along_ctx(tok[-1:], 1)
    tok_prev = jnp.concatenate([before, tok[:-1]], 0)
    q3, k3 = swap_core(q2), swap_core(k2)
    u1 = swap_core(w_up)
    u2 = jnp.concatenate([low, high], 0)
    u3 = swap_core(u2)

    marks = bounds[0].astype(F32)[:, None]
    decay = jnp.pad(decay_rates, (0, LANES - heads))[None]
    flat, wide, narrow = (length, width), (length, hidden), (length, LANES)
    queries, keys, mix, keep, stats, local_adjoint, outs, b_message = call(
        rates_kernel,
        [(flat, F32), (flat, F32), (narrow, F32), (narrow, F32), (narrow, F32), (wide, F32),
         ((blocks, hidden), F32), ((RANGES, 2, hidden), F32)],
        [pltpu.VMEM((width, width), BF16), pltpu.VMEM((width, width), BF16),
         pltpu.VMEM((2, hidden), F32)],
        8_000_000_000,
        place, tok, tok_prev, marks, decay, cot,
        w_query, q1, q2, q3, w_key, k1, k2, k3,
    )
    b_messages = lax.all_to_all(b_message, CTX, 0, 0, tiled=True)
    values, local_states, ins, f_message = call(
        states_kernel,
        [(wide, F32), (wide, F32), ((blocks, hidden), F32), ((RANGES, 1, hidden), F32)],
        [pltpu.VMEM((width, hidden), BF16), pltpu.VMEM((1, hidden), F32)],
        8_000_000_000,
        place, tok, mix, keep, w_up, u1, u2, u3,
    )
    f_messages = lax.all_to_all(f_message, CTX, 0, 0, tiled=True)
    adjoint, d_values = call(
        adjoint_kernel,
        [(wide, F32), (wide, BF16)],
        [],
        3_000_000_000,
        place, local_adjoint, outs, mix, keep, b_messages,
    )

    def cols(t, which):
        return jnp.concatenate(
            [lax.dynamic_slice_in_dim(t, (2 * b + which) * rows, rows, 1) for b in range(2)], 1
        )

    def share(which, d, source):
        return lax.dot_general(
            cols(source, which), d, (((0,), (0,)), ((), ())), preferred_element_type=F32
        )

    def paired(d, source):
        theirs = swap_core(share(1 - core, d, source).astype(BF16))
        return (share(core, d, source) + theirs.astype(F32)).astype(BF16)

    up_sum = paired(d_values, tok)
    dechunked, d_query, d_prev = call(
        router_kernel,
        [(wide, BF16), (flat, BF16), (flat, BF16)],
        [],
        3_000_000_000,
        place, local_states, ins, keep, stats, decay, f_messages, b_messages, values, adjoint,
        queries, keys,
    )
    q_sum, k_sum = paired(d_query, tok), paired(d_prev, tok_prev)
    pair_sum = jnp.concatenate([q_sum, k_sum, up_sum], 1)
    exchanged = lax.all_to_all(
        pair_sum.reshape(64, -1, pair_sum.shape[1]), ("xl", "dp", "z", "xh"), 0, 0, tiled=True
    )
    total = jnp.sum(exchanged.astype(F32), 0).astype(BF16)
    summed = spread(total, ("dp", "z", "xh"), 32).reshape(rows, -1).astype(F32)

    d_key = jnp.concatenate([d_prev[1:], along_ctx(d_prev[:1], -1)], 0)
    (grad_tokens,) = call(
        tokens_kernel,
        [(flat, BF16)],
        [],
        5_000_000_000,
        place, d_query, d_key, d_values,
        w_query, w_key, w_up, q1, k1, u1, q2, k2, u2, q3, k3, u3,
    )
    return (
        dechunked[None],
        grad_tokens[None],
        summed[:, :width],
        summed[:, width : 2 * width],
        summed[:, 2 * width :],
    )


def solution(mesh):
    split = jax.sharding.Mesh(
        mesh.devices.reshape(4, 2, 2, 4, 2), ("dp", "xl", "core", "z", "xh")
    )
    rows = P(("xl", "core"), None)
    data = P(("dp", "xl", "core"), CTX, None)
    return jax.shard_map(
        per_device,
        mesh=split,
        in_specs=(data, P(("dp", "xl", "core"), CTX), P(), rows, rows, rows, data),
        out_specs=(data, data, rows, rows, rows),
        check_vma=False,
    )
```

```python
import functools

import jax
import jax.numpy as jnp
from jax import lax
from jax.experimental import pallas as pl
from jax.experimental.pallas import tpu as pltpu
from jax.sharding import PartitionSpec as P

SPAN = 128
LANES = 128
epsilon = 1e-06
CTX = ("z", "xh")
RANGES = 8
HIGHEST = lax.Precision.HIGHEST
F32 = jnp.float32
BF16 = jnp.bfloat16


def along_x(a, by):
    pairs = []
    for xl in range(2):
        for xh in range(2):
            x = (xh * 2 + xl + by) % 4
            pairs.append((xl * 2 + xh, (x % 2) * 2 + x // 2))
    return lax.ppermute(a, ("xl", "xh"), pairs)


def swap_core(a):
    return lax.ppermute(a, "core", [(0, 1), (1, 0)])


def along_ctx(a, by):
    return lax.ppermute(
        a, CTX, [(i, i + by) for i in range(RANGES) if 0 <= i + by < RANGES]
    )


def spread(a, axes, count):
    return lax.all_to_all(jnp.broadcast_to(a[None], (count,) + a.shape), axes, 0, 0, tiled=True)


def mxu(a, b):
    return jnp.dot(a, b, preferred_element_type=F32)


def halves(a):
    high = a.astype(BF16)
    return high, (a - high.astype(F32)).astype(BF16)


def ids(shape, dim):
    return lax.broadcasted_iota(jnp.int32, shape, dim)


def head_cols(h):
    return slice(h * LANES, (h + 1) * LANES)


def span(n):
    return pl.ds(pl.multiple_of(n * SPAN, SPAN), SPAN)


def fetch_panel(place, pieces, whole, sems):
    rows = whole.shape[0] // 4
    copies = []
    for j, piece in enumerate(pieces):
        at = pl.multiple_of((place[0] ^ (j // (len(pieces) // 4))) * rows, rows)
        part = piece.shape[0]
        start = at + (j % (len(pieces) // 4)) * part
        copies.append(
            pltpu.make_async_copy(
                piece, whole.at[pl.ds(pl.multiple_of(start, part), part), :], sems.at[j]
            )
        )
    return copies


def block_copy(source, target, sems, n):
    return pltpu.make_async_copy(source.at[span(n), :], target.at[span(n), :], sems.at[n])


def whole_copy(source, target, sem):
    return pltpu.make_async_copy(source, target, sem)


def rates_kernel(
    place, tok, tok_prev, bounds, decay, cot, q0, q1, q2, q3, k0, k1, k2, k3,
    queries_out, keys_out, adjoint_out, mix_out, keep_out, stats_out, outs, message,
    wq, wk, carry, queries, keys, adjoint, q_sems, k_sems, a_sems, sems,
):
    hidden = adjoint.shape[1]
    heads = hidden // LANES
    blocks = adjoint.shape[0] // SPAN
    load_q = fetch_panel(place, (q0, q1, q2, q3), wq, q_sems)
    load_k = fetch_panel(place, (k0, k1, k2, k3), wk, k_sems)
    for c in load_q + load_k:
        c.start()
    carry[0:1, :] = jnp.zeros((1, hidden), F32)
    carry[1:2, :] = jnp.ones((1, hidden), F32)
    for c in load_q:
        c.wait()
    queries[...] = mxu(tok[...], wq[...])
    save_q = whole_copy(queries, queries_out, sems.at[0])
    save_q.start()
    for c in load_k:
        c.wait()
    keys[...] = mxu(tok_prev[...], wk[...])
    save_k = whole_copy(keys, keys_out, sems.at[1])
    save_k.start()

    @pl.loop(0, blocks)
    def _(step):
        n = blocks - 1 - step
        rows = span(n)
        q, k = queries[rows, :], keys[rows, :]
        iq = lax.rsqrt(jnp.sum(q * q, -1, keepdims=True) + epsilon)
        ik = lax.rsqrt(jnp.sum(k * k, -1, keepdims=True) + epsilon)
        cosine = jnp.sum(q * k, -1, keepdims=True) * iq * ik
        lane = ids((SPAN, LANES), 1)
        sub = ids((SPAN, LANES), 0)
        first = jnp.logical_and(place[1] == 0, n == 0)
        opening = jnp.logical_and(first, ids((SPAN, 1), 0) == 0)
        prob = jnp.where(opening, 1.0, 0.5 * (1.0 - cosine))
        marked = jnp.where(opening, 1.0, bounds[rows, :])
        mix = (marked * prob) * decay[...]
        logs = jnp.log(1.0 - mix)
        lower = (sub >= lane).astype(F32)
        keep = jnp.dot(lower, logs, precision=HIGHEST, preferred_element_type=F32)
        keep_rows = keep.T
        active = jnp.where(opening, 0.0, marked)
        stats = jnp.where(
            lane == 0, iq, jnp.where(lane == 1, ik, jnp.where(lane == 2, cosine, active))
        )
        mix_out[rows, :] = mix
        keep_out[rows, :] = keep
        stats_out[rows, :] = stats
        outs[pl.ds(n, 1), :] = carry[0:1, :]
        total = jnp.exp(keep[SPAN - 1 : SPAN, :])
        upper = sub <= lane
        for h in range(heads):
            cols = head_cols(h)
            gap = keep_rows[h : h + 1, :] - keep[:, h : h + 1]
            band = jnp.where(upper, jnp.exp(jnp.where(upper, gap, 0.0)), 0.0)
            high, low = halves(band)
            g = cot[rows, cols]
            local = mxu(high, g) + mxu(low, g)
            adjoint[rows, cols] = local
            d = total[:, h : h + 1]
            carry[0:1, cols] = d * carry[0:1, cols] + (1.0 - mix[0:1, h : h + 1]) * local[0:1, :]
            carry[1:2, cols] = d * carry[1:2, cols]
        block_copy(adjoint, adjoint_out, a_sems, n).start()

    for j in range(RANGES):
        message[j] = carry[...]
    save_q.wait()
    save_k.wait()
    for n in range(blocks):
        block_copy(adjoint, adjoint_out, a_sems, n).wait()


def states_kernel(
    place, tok, mix_ref, keep_ref, u0, u1, u2, u3, u4, u5, u6, u7,
    values_out, states_out, ins, message,
    wu, carry, values, states, u_sems, s_sems, sems,
):
    hidden = values.shape[1]
    heads = hidden // LANES
    blocks = values.shape[0] // SPAN
    loads = fetch_panel(place, (u0, u1, u2, u3, u4, u5, u6, u7), wu, u_sems)
    for c in loads:
        c.start()
    carry[...] = jnp.zeros_like(carry)
    for c in loads:
        c.wait()
    values[...] = mxu(tok[...], wu[...])
    save_v = whole_copy(values, values_out, sems.at[0])
    save_v.start()

    @pl.loop(0, blocks)
    def _(n):
        rows = span(n)
        mix, keep = mix_ref[rows, :], keep_ref[rows, :]
        keep_rows = keep.T
        lower = ids((SPAN, LANES), 0) >= ids((SPAN, LANES), 1)
        ins[pl.ds(n, 1), :] = carry[0:1, :]
        total = jnp.exp(keep[SPAN - 1 : SPAN, :])
        for h in range(heads):
            cols = head_cols(h)
            gap = keep[:, h : h + 1] - keep_rows[h : h + 1, :]
            band = jnp.where(lower, jnp.exp(jnp.where(lower, gap, 0.0)), 0.0)
            high, low = halves(band)
            added, rest = halves(mix[:, h : h + 1] * values[rows, cols])
            local = mxu(high, added) + mxu(low, added) + mxu(high, rest)
            states[rows, cols] = local
            carry[0:1, cols] = total[:, h : h + 1] * carry[0:1, cols] + local[SPAN - 1 : SPAN, :]
        block_copy(states, states_out, s_sems, n).start()

    for j in range(RANGES):
        message[j] = carry[...]
    save_v.wait()
    for n in range(blocks):
        block_copy(states, states_out, s_sems, n).wait()


def adjoint_in(own, messages):
    incoming = jnp.zeros((1, messages.shape[2]), F32)
    for j in reversed(range(RANGES)):
        nearer = messages[j, 1:2, :] * incoming + messages[j, 0:1, :]
        incoming = jnp.where(j > own, nearer, incoming)
    return incoming


def adjoint_kernel(
    place, local_in, outs, mix_ref, keep_ref, messages, after_states,
    d_values_out, tails, local, d_values, in_sems, out_sems,
):
    heads = local.shape[1] // LANES
    blocks = local.shape[0] // SPAN
    for n in reversed(range(blocks)):
        block_copy(local_in, local, in_sems, n).start()
    incoming = adjoint_in(place[1], messages)

    def block(step, after):
        n = blocks - 1 - step
        rows = span(n)
        mix, keep = mix_ref[rows, :], keep_ref[rows, :]
        last = keep[SPAN - 1 : SPAN, :]
        fade = jnp.exp(last - keep)
        reach = jnp.exp(after)
        back = outs[pl.ds(n, 1), :]
        block_copy(local_in, local, in_sems, n).wait()
        ends = []
        for h in range(heads):
            cols = head_cols(h)
            tail = back[:, cols] + reach[:, h : h + 1] * incoming[:, cols]
            ends.append(tail)
            full = local[rows, cols] + fade[:, h : h + 1] * tail
            d_values[rows, cols] = (mix[:, h : h + 1] * full).astype(BF16)
        tails[pl.ds(n, 1), :] = jnp.concatenate(ends, 1)
        block_copy(d_values, d_values_out, out_sems, n).start()
        return after + last

    lax.fori_loop(0, blocks, block, jnp.zeros((1, LANES), F32))
    for n in range(blocks):
        block_copy(d_values, d_values_out, out_sems, n).wait()


def router_kernel(
    place, ins, tails, keep_ref, stats_ref, decay, messages, decays,
    local_in, values_in, adjoint_ref, queries_in, keys_in,
    dechunked_out, d_query_out, d_prev_out,
    local, values, adjoint, queries, keys, dechunked, d_query, d_prev,
    l_sems, v_sems, a_sems, q_sems, k_sems, d_sems, dq_sems, dp_sems,
):
    heads = values.shape[1] // LANES
    blocks = values.shape[0] // SPAN
    own = place[1]
    loads = (
        (local_in, local, l_sems), (values_in, values, v_sems), (adjoint_ref, adjoint, a_sems),
        (queries_in, queries, q_sems), (keys_in, keys, k_sems),
    )
    saves = (
        (dechunked, dechunked_out, d_sems), (d_query, d_query_out, dq_sems),
        (d_prev, d_prev_out, dp_sems),
    )
    for n in range(blocks):
        for source, target, sem in loads:
            block_copy(source, target, sem, n).start()
    incoming = jnp.zeros((1, values.shape[1]), F32)
    for j in range(RANGES):
        nearer = decays[j, 1:2, :] * incoming + messages[j, 0:1, :]
        incoming = jnp.where(j < own, nearer, incoming)

    def block(n, before):
        rows = span(n)
        keep = keep_ref[rows, :]
        fade = jnp.exp(keep)
        last = keep[SPAN - 1 : SPAN, :]
        fade_back = jnp.exp(last - keep)
        reach = jnp.exp(before)
        start = ins[pl.ds(n, 1), :]
        tail = tails[pl.ds(n, 1), :]
        top = ids((SPAN, LANES), 0) == 0
        total = jnp.zeros((SPAN, LANES), F32)
        for source, target, sem in loads:
            block_copy(source, target, sem, n).wait()
        for h in range(heads):
            cols = head_cols(h)
            base = start[:, cols] + reach[:, h : h + 1] * incoming[:, cols]
            state = local[rows, cols] + fade[:, h : h + 1] * base
            dechunked[rows, cols] = state.astype(BF16)
            earlier = jnp.where(top, base, pltpu.roll(state, 1, 0))
            full = adjoint[rows, cols] + fade_back[:, h : h + 1] * tail[:, cols]
            total = total + (decay[:, h : h + 1] * full) * (values[rows, cols] - earlier)
        stats = stats_ref[rows, :]
        iq, ik, cosine, active = (stats[:, i : i + 1] for i in range(4))
        d_cos = -0.5 * (active * jnp.sum(total, -1, keepdims=True))
        both = d_cos * (iq * ik)
        over_q, over_k = d_cos * (cosine * iq * iq), d_cos * (cosine * ik * ik)
        q, k = queries[rows, :], keys[rows, :]
        d_query[rows, :] = (k * both - over_q * q).astype(BF16)
        d_prev[rows, :] = (q * both - over_k * k).astype(BF16)
        for source, target, sem in saves:
            block_copy(source, target, sem, n).start()
        return before + last

    lax.fori_loop(0, blocks, block, jnp.zeros((1, LANES), F32))
    for n in range(blocks):
        for source, target, sem in saves:
            block_copy(source, target, sem, n).wait()


def tokens_kernel(place, d_query_in, d_key_in, d_values_in, *refs):
    pieces, out = refs[:16], refs[16]
    d_query, d_key, d_values, wq, wk, wu, d_sems, q_sems, k_sems, u_sems = refs[17:]
    loads = [
        whole_copy(source, target, d_sems.at[i])
        for i, (source, target) in enumerate(
            ((d_query_in, d_query), (d_key_in, d_key), (d_values_in, d_values))
        )
    ]
    loads += fetch_panel(place, pieces[:4], wq, q_sems)
    loads += fetch_panel(place, pieces[4:8], wk, k_sems)
    loads += fetch_panel(place, pieces[8:], wu, u_sems)
    for c in loads:
        c.start()
    for c in loads:
        c.wait()
    dims = (((1,), (1,)), ((), ()))
    rows = wq.shape[0] // 4
    for j in range(4):
        part = slice(j * rows, (j + 1) * rows)
        terms = [
            lax.dot_general(d[...], w[part, :], dims, preferred_element_type=F32)
            for d, w in ((d_query, wq), (d_key, wk), (d_values, wu))
        ]
        out[:, part] = (terms[0] + terms[1] + terms[2]).astype(BF16)


SMEM = pl.BlockSpec(memory_space=pltpu.SMEM)
VMEM = pl.BlockSpec(memory_space=pltpu.VMEM)
HBM = pl.BlockSpec(memory_space=pltpu.HBM)
DMA = pltpu.SemaphoreType.DMA
VMEM_LIMIT = 62 << 20


def call(body, vmem_args, hbm_args, hbm_outs, vmem_outs, scratch, flops):
    args = list(vmem_args) + list(hbm_args)
    outs = list(hbm_outs) + list(vmem_outs)
    return pl.pallas_call(
        body,
        out_shape=[jax.ShapeDtypeStruct(s, t) for s, t in outs],
        in_specs=[SMEM] + [VMEM] * (len(vmem_args) - 1) + [HBM] * len(hbm_args),
        out_specs=[HBM] * len(hbm_outs) + [VMEM] * len(vmem_outs),
        scratch_shapes=scratch,
        cost_estimate=pl.CostEstimate(flops=flops, bytes_accessed=1 << 20, transcendentals=0),
        compiler_params=pltpu.CompilerParams(vmem_limit_bytes=VMEM_LIMIT),
    )(*args)


def per_device(tokens, bounds, decay_rates, w_query, w_key, w_up, grad_out):
    _, length, width = tokens.shape
    hidden = w_up.shape[1]
    heads = decay_rates.shape[0]
    rows = w_query.shape[0]
    blocks = length // SPAN
    tok, cot = tokens[0], grad_out[0]
    core = lax.axis_index("core")
    place = jnp.stack([lax.axis_index("xl") * 2 + core, lax.axis_index(CTX)]).astype(jnp.int32)

    q2, k2 = along_x(w_query, -1), along_x(w_key, 1)
    q1, k1 = swap_core(w_query), swap_core(w_key)
    before = along_ctx(tok[-1:], 1)
    tok_prev = jnp.concatenate([before, tok[:-1]], 0)
    half = rows // 2
    up = (w_up[:half], w_up[half:])
    up_low, up_high, q2, k2 = lax.optimization_barrier((*up, q2, k2))
    q3, k3 = swap_core(q2), swap_core(k2)
    u2 = (along_x(up_low, -1), along_x(up_high, 1))
    u1 = tuple(swap_core(u) for u in up)

    marks = bounds[0].astype(F32)[:, None]
    decay = jnp.pad(decay_rates, (0, LANES - heads))[None]
    flat, wide, narrow = (length, width), (length, hidden), (length, LANES)
    square, tall, per_block = (width, width), (width, hidden), (blocks, hidden)
    buf = pltpu.VMEM
    queries, keys, local_adjoint, mix, keep, stats, outs, b_message = call(
        rates_kernel,
        (place, tok, tok_prev, marks, decay, cot),
        (w_query, q1, q2, q3, w_key, k1, k2, k3),
        ((flat, F32), (flat, F32), (wide, F32)),
        ((narrow, F32), (narrow, F32), (narrow, F32), (per_block, F32), ((RANGES, 2, hidden), F32)),
        [buf(square, BF16), buf(square, BF16), buf((2, hidden), F32), buf(flat, F32),
         buf(flat, F32), buf(wide, F32), DMA((4,)), DMA((4,)), DMA((blocks,)), DMA((2,))],
        8_000_000_000,
    )
    b_messages = lax.all_to_all(b_message, CTX, 0, 0, tiled=True)
    u2_low, u2_high, keep_late = lax.optimization_barrier((*u2, keep))
    u3 = (swap_core(u2_low), swap_core(u2_high))
    values, local_states, ins, f_message = call(
        states_kernel,
        (place, tok, mix, keep_late),
        (*up, *u1, u2_low, u2_high, *u3),
        ((wide, F32), (wide, F32)),
        ((per_block, F32), ((RANGES, 1, hidden), F32)),
        [buf(tall, BF16), buf((1, hidden), F32), buf(wide, F32), buf(wide, F32),
         DMA((8,)), DMA((blocks,)), DMA((1,))],
        8_000_000_000,
    )
    f_messages = lax.all_to_all(f_message, CTX, 0, 0, tiled=True)
    d_values, tails = pl.pallas_call(
        adjoint_kernel,
        out_shape=[jax.ShapeDtypeStruct(wide, BF16), jax.ShapeDtypeStruct(per_block, F32)],
        in_specs=[SMEM, HBM, VMEM, VMEM, VMEM, VMEM, HBM],
        out_specs=[HBM, VMEM],
        scratch_shapes=[buf(wide, F32), buf(wide, BF16), DMA((blocks,)), DMA((blocks,))],
        cost_estimate=pl.CostEstimate(flops=3_000_000_000, bytes_accessed=1 << 20, transcendentals=0),
        compiler_params=pltpu.CompilerParams(vmem_limit_bytes=VMEM_LIMIT),
    )(place, local_adjoint, outs, mix, keep, b_messages, values)

    def cols(t, which):
        return jnp.concatenate(
            [lax.dynamic_slice_in_dim(t, (2 * b + which) * rows, rows, 1) for b in range(2)], 1
        ).T

    now = {side: cols(tok, abs(side - core)) for side in (0, 1)}
    prev = {side: cols(tok_prev, abs(side - core)) for side in (0, 1)}

    def paired(d, source):
        theirs = swap_core(mxu(source[1], d).astype(BF16))
        return (mxu(source[0], d) + theirs.astype(F32)).astype(BF16)

    up_sum = paired(d_values, now)
    dechunked, d_query, d_prev = call(
        router_kernel,
        (place, ins, tails, keep, stats, decay, f_messages, b_messages),
        (local_states, values, local_adjoint, queries, keys),
        ((wide, BF16), (flat, BF16), (flat, BF16)),
        (),
        [buf(wide, F32), buf(wide, F32), buf(wide, F32), buf(flat, F32), buf(flat, F32),
         buf(wide, BF16), buf(flat, BF16), buf(flat, BF16)] + [DMA((blocks,))] * 8,
        3_000_000_000,
    )
    after = along_ctx(d_prev[:1], -1)
    q_sum, k_sum = paired(d_query, now), paired(d_prev, prev)
    pair_sum = jnp.concatenate([q_sum, k_sum, up_sum], 1)
    pair_sum, after = lax.optimization_barrier((pair_sum, after))
    exchanged = lax.all_to_all(
        pair_sum.reshape(64, -1, pair_sum.shape[1]), ("xl", "dp", "z", "xh"), 0, 0, tiled=True
    )
    total = jnp.sum(exchanged.astype(F32), 0).astype(BF16)
    summed = spread(total, ("dp", "z", "xh"), 32)

    d_key = jnp.concatenate([d_prev[1:], after], 0)
    (grad_tokens,) = call(
        tokens_kernel,
        (place,),
        (d_query, d_key, d_values, w_query, q1, q2, q3, w_key, k1, k2, k3,
         *up, *u1, u2_low, u2_high, *u3),
        (),
        ((flat, BF16),),
        [buf(flat, BF16), buf(flat, BF16), buf(wide, BF16), buf(square, BF16), buf(square, BF16),
         buf(tall, BF16), DMA((3,)), DMA((4,)), DMA((4,)), DMA((8,))],
        5_000_000_000,
    )
    grads = [
        summed[:, :, a:b].reshape(rows, b - a).astype(F32)
        for a, b in ((0, width), (width, 2 * width), (2 * width, 2 * width + hidden))
    ]
    return (dechunked[None], grad_tokens[None], *grads)


def solution(mesh):
    split = jax.sharding.Mesh(
        mesh.devices.reshape(4, 2, 2, 4, 2), ("dp", "xl", "core", "z", "xh")
    )
    rows = P(("xl", "core"), None)
    data = P(("dp", "xl", "core"), CTX, None)
    return jax.shard_map(
        per_device,
        mesh=split,
        in_specs=(data, P(("dp", "xl", "core"), CTX), P(), rows, rows, rows, data),
        out_specs=(data, data, rows, rows, rows),
        check_vma=False,
    )
```

```python
import functools

import jax
import jax.numpy as jnp
from jax import lax
from jax.experimental import pallas as pl
from jax.experimental.pallas import tpu as pltpu
from jax.sharding import PartitionSpec as P

SPAN = 128
LANES = 128
epsilon = 1e-06
CTX = ("z", "xh")
RANGES = 8
HIGHEST = lax.Precision.HIGHEST
F32 = jnp.float32
BF16 = jnp.bfloat16


def along_x(a, by):
    pairs = []
    for xl in range(2):
        for xh in range(2):
            x = (xh * 2 + xl + by) % 4
            pairs.append((xl * 2 + xh, (x % 2) * 2 + x // 2))
    return lax.ppermute(a, ("xl", "xh"), pairs)


def swap_core(a):
    return lax.ppermute(a, "core", [(0, 1), (1, 0)])


def along_ctx(a, by):
    return lax.ppermute(
        a, CTX, [(i, i + by) for i in range(RANGES) if 0 <= i + by < RANGES]
    )


def mxu(a, b):
    return jnp.dot(a, b, preferred_element_type=F32)


def halves(a):
    high = a.astype(BF16)
    return high, (a - high.astype(F32)).astype(BF16)


def ids(shape, dim):
    return lax.broadcasted_iota(jnp.int32, shape, dim)


def head_cols(h):
    return slice(h * LANES, (h + 1) * LANES)


def span(n):
    return pl.ds(pl.multiple_of(n * SPAN, SPAN), SPAN)


def fetch_panel(place, pieces, whole, sems):
    rows = whole.shape[0] // 4
    copies = []
    for j, piece in enumerate(pieces):
        at = pl.multiple_of((place[0] ^ (j // (len(pieces) // 4))) * rows, rows)
        part = piece.shape[0]
        start = at + (j % (len(pieces) // 4)) * part
        copies.append(
            pltpu.make_async_copy(
                piece, whole.at[pl.ds(pl.multiple_of(start, part), part), :], sems.at[j]
            )
        )
    return copies


def block_copy(source, target, sems, n):
    return pltpu.make_async_copy(source.at[span(n), :], target.at[span(n), :], sems.at[n])


def whole_copy(source, target, sem):
    return pltpu.make_async_copy(source, target, sem)


def rates_kernel(
    place, bounds, decay, tok_in, prev_in, cot_in, q0, q1, q2, q3, k0, k1, k2, k3,
    queries_out, keys_out, adjoint_out, mix_out, keep_out, stats_out, outs, message,
    wq, wk, carry, queries, keys, adjoint, tok, tok_prev, cot, q_sems, k_sems, a_sems, sems,
):
    hidden = adjoint.shape[1]
    heads = hidden // LANES
    blocks = adjoint.shape[0] // SPAN
    load_q = fetch_panel(place, (q0, q1, q2, q3), wq, q_sems)
    load_k = fetch_panel(place, (k0, k1, k2, k3), wk, k_sems)
    load_q.append(whole_copy(tok_in, tok, sems.at[2]))
    load_k.append(whole_copy(prev_in, tok_prev, sems.at[3]))
    load_cot = whole_copy(cot_in, cot, sems.at[4])
    for c in load_q + load_k:
        c.start()
    load_cot.start()
    carry[0:1, :] = jnp.zeros((1, hidden), F32)
    carry[1:2, :] = jnp.ones((1, hidden), F32)
    for c in load_q:
        c.wait()
    queries[...] = mxu(tok[...], wq[...])
    save_q = whole_copy(queries, queries_out, sems.at[0])
    save_q.start()
    for c in load_k:
        c.wait()
    keys[...] = mxu(tok_prev[...], wk[...])
    save_k = whole_copy(keys, keys_out, sems.at[1])
    save_k.start()
    load_cot.wait()

    @pl.loop(0, blocks)
    def _(step):
        n = blocks - 1 - step
        rows = span(n)
        q, k = queries[rows, :], keys[rows, :]
        iq = lax.rsqrt(jnp.sum(q * q, -1, keepdims=True) + epsilon)
        ik = lax.rsqrt(jnp.sum(k * k, -1, keepdims=True) + epsilon)
        cosine = jnp.sum(q * k, -1, keepdims=True) * iq * ik
        lane = ids((SPAN, LANES), 1)
        sub = ids((SPAN, LANES), 0)
        first = jnp.logical_and(place[1] == 0, n == 0)
        opening = jnp.logical_and(first, ids((SPAN, 1), 0) == 0)
        prob = jnp.where(opening, 1.0, 0.5 * (1.0 - cosine))
        marked = jnp.where(opening, 1.0, bounds[rows, :])
        mix = (marked * prob) * decay[...]
        logs = jnp.log(1.0 - mix)
        lower = (sub >= lane).astype(F32)
        keep = jnp.dot(lower, logs, precision=HIGHEST, preferred_element_type=F32)
        keep_rows = keep.T
        active = jnp.where(opening, 0.0, marked)
        stats = jnp.where(
            lane == 0, iq, jnp.where(lane == 1, ik, jnp.where(lane == 2, cosine, active))
        )
        mix_out[rows, :] = mix
        keep_out[rows, :] = keep
        stats_out[rows, :] = stats
        outs[pl.ds(n, 1), :] = carry[0:1, :]
        total = jnp.exp(keep[SPAN - 1 : SPAN, :])
        upper = sub <= lane
        for h in range(heads):
            cols = head_cols(h)
            gap = keep_rows[h : h + 1, :] - keep[:, h : h + 1]
            band = jnp.where(upper, jnp.exp(jnp.where(upper, gap, 0.0)), 0.0)
            high, low = halves(band)
            g = cot[rows, cols]
            local = mxu(high, g) + mxu(low, g)
            adjoint[rows, cols] = local
            d = total[:, h : h + 1]
            carry[0:1, cols] = d * carry[0:1, cols] + (1.0 - mix[0:1, h : h + 1]) * local[0:1, :]
            carry[1:2, cols] = d * carry[1:2, cols]
        block_copy(adjoint, adjoint_out, a_sems, n).start()

    for j in range(RANGES):
        message[j] = carry[...]
    save_q.wait()
    save_k.wait()
    for n in range(blocks):
        block_copy(adjoint, adjoint_out, a_sems, n).wait()


def states_kernel(
    place, mix_ref, keep_ref, tok_in, u0, u1, u2, u3, u4, u5, u6, u7,
    values_out, states_out, ins, message,
    wu, carry, values, states, tok, u_sems, s_sems, sems,
):
    hidden = values.shape[1]
    heads = hidden // LANES
    blocks = values.shape[0] // SPAN
    pieces = (u0, u1, u2, u3, u4, u5, u6, u7)
    near, far = slice(0, hidden // 2), slice(hidden // 2, hidden)
    load_tok = whole_copy(tok_in, tok, sems.at[2])
    loads = [
        fetch_panel(place, [u.at[:, part] for u in pieces], wu.at[:, part], u_sems.at[i])
        for i, part in enumerate((near, far))
    ]
    load_tok.start()
    for c in loads[0] + loads[1]:
        c.start()
    carry[...] = jnp.zeros_like(carry)
    load_tok.wait()
    save_v = []
    for i, part in enumerate((near, far)):
        for c in loads[i]:
            c.wait()
        values[:, part] = mxu(tok[...], wu[:, part])
        save_v.append(whole_copy(values.at[:, part], values_out.at[:, part], sems.at[i]))
        save_v[i].start()

    @pl.loop(0, blocks)
    def _(n):
        rows = span(n)
        mix, keep = mix_ref[rows, :], keep_ref[rows, :]
        keep_rows = keep.T
        lower = ids((SPAN, LANES), 0) >= ids((SPAN, LANES), 1)
        ins[pl.ds(n, 1), :] = carry[0:1, :]
        total = jnp.exp(keep[SPAN - 1 : SPAN, :])
        for h in range(heads):
            cols = head_cols(h)
            gap = keep[:, h : h + 1] - keep_rows[h : h + 1, :]
            band = jnp.where(lower, jnp.exp(jnp.where(lower, gap, 0.0)), 0.0)
            high, low = halves(band)
            added, rest = halves(mix[:, h : h + 1] * values[rows, cols])
            local = mxu(high, added) + mxu(low, added) + mxu(high, rest)
            states[rows, cols] = local
            carry[0:1, cols] = total[:, h : h + 1] * carry[0:1, cols] + local[SPAN - 1 : SPAN, :]
        block_copy(states, states_out, s_sems, n).start()

    for j in range(RANGES):
        message[j] = carry[...]
    for c in save_v:
        c.wait()
    for n in range(blocks):
        block_copy(states, states_out, s_sems, n).wait()


def adjoint_in(own, messages):
    incoming = jnp.zeros((1, messages.shape[2]), F32)
    for j in reversed(range(RANGES)):
        nearer = messages[j, 1:2, :] * incoming + messages[j, 0:1, :]
        incoming = jnp.where(j > own, nearer, incoming)
    return incoming


def partner_columns(place, source, target, sems):
    rows = target.shape[1] // 2
    copies = []
    for b in range(2):
        start = pl.multiple_of((2 * b + 1 - place[0] % 2) * rows, rows)
        copies.append(
            pltpu.make_async_copy(
                source.at[:, pl.ds(start, rows)],
                target.at[:, b * rows : (b + 1) * rows],
                sems.at[b],
            )
        )
    return copies


def shares(lhs, d, share, share_out, sems):
    step = 512
    saves = []
    for i in range(d.shape[1] // step):
        part = slice(i * step, (i + 1) * step)
        share[:, part] = lax.dot_general(
            lhs[...], d[:, part], (((0,), (0,)), ((), ())), preferred_element_type=F32
        ).astype(BF16)
        saves.append(whole_copy(share.at[:, part], share_out.at[:, part], sems.at[i]))
        saves[i].start()
    return saves


def adjoint_kernel(
    place, outs, mix_ref, keep_ref, messages, local_in, theirs_in, after_states,
    d_values_out, share_out, tails, local, d_values, theirs, share, in_sems, out_sems, s_sems,
    t_sems,
):
    heads = local.shape[1] // LANES
    blocks = local.shape[0] // SPAN
    for n in reversed(range(blocks)):
        block_copy(local_in, local, in_sems, n).start()
    sides = partner_columns(place, theirs_in, theirs, t_sems)
    for c in sides:
        c.start()
    incoming = adjoint_in(place[1], messages)

    def block(step, after):
        n = blocks - 1 - step
        rows = span(n)
        mix, keep = mix_ref[rows, :], keep_ref[rows, :]
        last = keep[SPAN - 1 : SPAN, :]
        fade = jnp.exp(last - keep)
        reach = jnp.exp(after)
        back = outs[pl.ds(n, 1), :]
        block_copy(local_in, local, in_sems, n).wait()
        ends = []
        for h in range(heads):
            cols = head_cols(h)
            tail = back[:, cols] + reach[:, h : h + 1] * incoming[:, cols]
            ends.append(tail)
            full = local[rows, cols] + fade[:, h : h + 1] * tail
            d_values[rows, cols] = (mix[:, h : h + 1] * full).astype(BF16)
        tails[pl.ds(n, 1), :] = jnp.concatenate(ends, 1)
        block_copy(d_values, d_values_out, out_sems, n).start()
        return after + last

    lax.fori_loop(0, blocks, block, jnp.zeros((1, LANES), F32))
    for c in sides:
        c.wait()
    saves = shares(theirs, d_values, share, share_out, s_sems)
    for c in saves:
        c.wait()
    for n in range(blocks):
        block_copy(d_values, d_values_out, out_sems, n).wait()


def router_kernel(
    place, ins, tails, keep_ref, stats_ref, decay, messages, decays,
    local_in, values_in, adjoint_ref, queries_in, keys_in, now_in, prev_in,
    dechunked_out, d_query_out, d_prev_out, q_share_out, k_share_out,
    local, values, adjoint, queries, keys, dechunked, d_query, d_prev, now, prev, q_share, k_share,
    l_sems, v_sems, a_sems, q_sems, k_sems, d_sems, dq_sems, dp_sems, qs_sems, ks_sems, t_sems,
):
    heads = values.shape[1] // LANES
    blocks = values.shape[0] // SPAN
    own = place[1]
    loads = (
        (local_in, local, l_sems), (values_in, values, v_sems), (adjoint_ref, adjoint, a_sems),
        (queries_in, queries, q_sems), (keys_in, keys, k_sems),
    )
    saves = (
        (dechunked, dechunked_out, d_sems), (d_query, d_query_out, dq_sems),
        (d_prev, d_prev_out, dp_sems),
    )
    for n in range(blocks):
        for source, target, sem in loads:
            block_copy(source, target, sem, n).start()
    sides = partner_columns(place, now_in, now, t_sems.at[0])
    sides += partner_columns(place, prev_in, prev, t_sems.at[1])
    for c in sides:
        c.start()
    incoming = jnp.zeros((1, values.shape[1]), F32)
    for j in range(RANGES):
        nearer = decays[j, 1:2, :] * incoming + messages[j, 0:1, :]
        incoming = jnp.where(j < own, nearer, incoming)

    def block(n, before):
        rows = span(n)
        keep = keep_ref[rows, :]
        fade = jnp.exp(keep)
        last = keep[SPAN - 1 : SPAN, :]
        fade_back = jnp.exp(last - keep)
        reach = jnp.exp(before)
        start = ins[pl.ds(n, 1), :]
        tail = tails[pl.ds(n, 1), :]
        top = ids((SPAN, LANES), 0) == 0
        total = jnp.zeros((SPAN, LANES), F32)
        for source, target, sem in loads:
            block_copy(source, target, sem, n).wait()
        for h in range(heads):
            cols = head_cols(h)
            base = start[:, cols] + reach[:, h : h + 1] * incoming[:, cols]
            state = local[rows, cols] + fade[:, h : h + 1] * base
            dechunked[rows, cols] = state.astype(BF16)
            earlier = jnp.where(top, base, pltpu.roll(state, 1, 0))
            full = adjoint[rows, cols] + fade_back[:, h : h + 1] * tail[:, cols]
            total = total + (decay[:, h : h + 1] * full) * (values[rows, cols] - earlier)
        stats = stats_ref[rows, :]
        iq, ik, cosine, active = (stats[:, i : i + 1] for i in range(4))
        d_cos = -0.5 * (active * jnp.sum(total, -1, keepdims=True))
        both = d_cos * (iq * ik)
        over_q, over_k = d_cos * (cosine * iq * iq), d_cos * (cosine * ik * ik)
        q, k = queries[rows, :], keys[rows, :]
        d_query[rows, :] = (k * both - over_q * q).astype(BF16)
        d_prev[rows, :] = (q * both - over_k * k).astype(BF16)
        for source, target, sem in saves:
            block_copy(source, target, sem, n).start()
        return before + last

    lax.fori_loop(0, blocks, block, jnp.zeros((1, LANES), F32))
    for c in sides:
        c.wait()
    out = shares(now, d_query, q_share, q_share_out, qs_sems)
    out += shares(prev, d_prev, k_share, k_share_out, ks_sems)
    for c in out:
        c.wait()
    for n in range(blocks):
        for source, target, sem in saves:
            block_copy(source, target, sem, n).wait()


def tokens_kernel(place, d_query_in, d_key_in, d_values_in, *refs):
    pieces, out = refs[:16], refs[16]
    d_query, d_key, d_values, wq, wk, wu, d_sems, q_sems, k_sems, u_sems = refs[17:]
    loads = [
        whole_copy(source, target, d_sems.at[i])
        for i, (source, target) in enumerate(
            ((d_query_in, d_query), (d_key_in, d_key), (d_values_in, d_values))
        )
    ]
    loads += fetch_panel(place, pieces[:4], wq, q_sems)
    loads += fetch_panel(place, pieces[4:8], wk, k_sems)
    loads += fetch_panel(place, pieces[8:], wu, u_sems)
    for c in loads:
        c.start()
    for c in loads:
        c.wait()
    dims = (((1,), (1,)), ((), ()))
    rows = wq.shape[0] // 4
    for j in range(4):
        part = slice(j * rows, (j + 1) * rows)
        terms = [
            lax.dot_general(d[...], w[part, :], dims, preferred_element_type=F32)
            for d, w in ((d_query, wq), (d_key, wk), (d_values, wu))
        ]
        out[:, part] = (terms[0] + terms[1] + terms[2]).astype(BF16)


def sum_kernel(parts, out, total):
    step = pl.program_id(0)

    @pl.when(step == 0)
    def _():
        total[...] = jnp.zeros_like(total)

    width = 1024
    for i in range(total.shape[1] // width):
        part = slice(i * width, (i + 1) * width)
        acc = total[:, part]
        for j in range(parts.shape[0]):
            acc = acc + parts[j, :, part].astype(F32)
        total[:, part] = acc

    @pl.when(step == pl.num_programs(0) - 1)
    def _():
        rounded = total[...].astype(BF16)
        for j in range(out.shape[0]):
            out[j] = rounded


def sum_ranks(exchanged, copies):
    ranks, depth, width = exchanged.shape
    group = 16
    return pl.pallas_call(
        sum_kernel,
        grid=(ranks // group,),
        out_shape=jax.ShapeDtypeStruct((copies, depth, width), BF16),
        in_specs=[pl.BlockSpec((group, depth, width), lambda i: (i, 0, 0))],
        out_specs=pl.BlockSpec((copies, depth, width), lambda i: (0, 0, 0)),
        scratch_shapes=[pltpu.VMEM((depth, width), F32)],
        compiler_params=pltpu.CompilerParams(vmem_limit_bytes=VMEM_LIMIT),
    )(exchanged)


def widen_kernel(parts, *outs):
    depth = parts.shape[1]
    for j in range(parts.shape[0]):
        start = 0
        for out in outs:
            width = out.shape[1]
            out[j * depth : (j + 1) * depth, :] = parts[j, :, start : start + width].astype(F32)
            start += width


def widen(summed, widths):
    ranks, depth, width = summed.shape
    group = 8
    return pl.pallas_call(
        widen_kernel,
        grid=(ranks // group,),
        out_shape=[jax.ShapeDtypeStruct((ranks * depth, w), F32) for w in widths],
        in_specs=[pl.BlockSpec((group, depth, width), lambda i: (i, 0, 0))],
        out_specs=[pl.BlockSpec((group * depth, w), lambda i: (i, 0)) for w in widths],
        compiler_params=pltpu.CompilerParams(vmem_limit_bytes=VMEM_LIMIT),
    )(summed)


SMEM = pl.BlockSpec(memory_space=pltpu.SMEM)
VMEM = pl.BlockSpec(memory_space=pltpu.VMEM)
HBM = pl.BlockSpec(memory_space=pltpu.HBM)
DMA = pltpu.SemaphoreType.DMA
VMEM_LIMIT = 62 << 20


def call(body, vmem_args, hbm_args, hbm_outs, vmem_outs, scratch, flops):
    args = list(vmem_args) + list(hbm_args)
    outs = list(hbm_outs) + list(vmem_outs)
    return pl.pallas_call(
        body,
        out_shape=[jax.ShapeDtypeStruct(s, t) for s, t in outs],
        in_specs=[SMEM] + [VMEM] * (len(vmem_args) - 1) + [HBM] * len(hbm_args),
        out_specs=[HBM] * len(hbm_outs) + [VMEM] * len(vmem_outs),
        scratch_shapes=scratch,
        cost_estimate=pl.CostEstimate(flops=flops, bytes_accessed=1 << 20, transcendentals=0),
        compiler_params=pltpu.CompilerParams(vmem_limit_bytes=VMEM_LIMIT),
    )(*args)


def per_device(tokens, bounds, decay_rates, w_query, w_key, w_up, grad_out):
    _, length, width = tokens.shape
    hidden = w_up.shape[1]
    heads = decay_rates.shape[0]
    rows = w_query.shape[0]
    blocks = length // SPAN
    tok, cot = tokens[0], grad_out[0]
    core = lax.axis_index("core")
    place = jnp.stack([lax.axis_index("xl") * 2 + core, lax.axis_index(CTX)]).astype(jnp.int32)

    q2, k2 = along_x(w_query, -1), along_x(w_key, 1)
    q1, k1 = swap_core(w_query), swap_core(w_key)
    before = along_ctx(tok[-1:], 1)
    tok_prev = jnp.concatenate([before, tok[:-1]], 0)
    half = rows // 2
    up = (w_up[:half], w_up[half:])
    up_low, up_high, q2 = lax.optimization_barrier((*up, q2))
    q3, k3 = swap_core(q2), swap_core(k2)
    u2 = (along_x(up_low, -1), along_x(up_high, 1))
    u1 = tuple(swap_core(u) for u in up)

    marks = bounds[0].astype(F32)[:, None]
    decay = jnp.pad(decay_rates, (0, LANES - heads))[None]
    flat, wide, narrow = (length, width), (length, hidden), (length, LANES)
    square, tall, per_block = (width, width), (width, hidden), (blocks, hidden)
    buf = pltpu.VMEM
    queries, keys, local_adjoint, mix, keep, stats, outs, b_message = call(
        rates_kernel,
        (place, marks, decay),
        (tok, tok_prev, cot, w_query, q1, q2, q3, w_key, k1, k2, k3),
        ((flat, F32), (flat, F32), (wide, F32)),
        ((narrow, F32), (narrow, F32), (narrow, F32), (per_block, F32), ((RANGES, 2, hidden), F32)),
        [buf(square, BF16), buf(square, BF16), buf((2, hidden), F32), buf(flat, F32),
         buf(flat, F32), buf(wide, F32), buf(flat, BF16), buf(flat, BF16), buf(wide, BF16),
         DMA((4,)), DMA((4,)), DMA((blocks,)), DMA((5,))],
        8_000_000_000,
    )
    b_messages = lax.all_to_all(b_message, CTX, 0, 0, tiled=True)
    u2_low, u2_high, keep_late = lax.optimization_barrier((*u2, keep))
    u3 = (swap_core(u2_low), swap_core(u2_high))
    values, local_states, ins, f_message = call(
        states_kernel,
        (place, mix, keep_late),
        (tok, *up, *u1, u2_low, u2_high, *u3),
        ((wide, F32), (wide, F32)),
        ((per_block, F32), ((RANGES, 1, hidden), F32)),
        [buf(tall, BF16), buf((1, hidden), F32), buf(wide, F32), buf(wide, F32), buf(flat, BF16),
         DMA((2, 8)), DMA((blocks,)), DMA((3,))],
        8_000_000_000,
    )
    f_messages = lax.all_to_all(f_message, CTX, 0, 0, tiled=True)
    def cols(t):
        return jnp.concatenate(
            [lax.dynamic_slice_in_dim(t, (2 * b + core) * rows, rows, 1) for b in range(2)], 1
        )

    side, half_flat, half_wide = (length, 2 * rows), (2 * rows, width), (2 * rows, hidden)
    d_values, up_share, tails = call(
        adjoint_kernel,
        (place, outs, mix, keep, b_messages),
        (local_adjoint, tok, values),
        ((wide, BF16), (half_wide, BF16)),
        ((per_block, F32),),
        [buf(wide, F32), buf(wide, BF16), buf(side, BF16), buf(half_wide, BF16), DMA((blocks,)),
         DMA((blocks,)), DMA((4,)), DMA((2,))],
        3_000_000_000,
    )
    up_share, f_messages = lax.optimization_barrier((up_share, f_messages))
    up_theirs = swap_core(up_share)
    dechunked, d_query, d_prev, q_share, k_share = call(
        router_kernel,
        (place, ins, tails, keep, stats, decay, f_messages, b_messages),
        (local_states, values, local_adjoint, queries, keys, tok, tok_prev),
        ((wide, BF16), (flat, BF16), (flat, BF16), (half_flat, BF16), (half_flat, BF16)),
        (),
        [buf(wide, F32), buf(wide, F32), buf(wide, F32), buf(flat, F32), buf(flat, F32),
         buf(wide, BF16), buf(flat, BF16), buf(flat, BF16), buf(side, BF16), buf(side, BF16),
         buf(half_flat, BF16), buf(half_flat, BF16)]
        + [DMA((blocks,))] * 8 + [DMA((2,)), DMA((2,)), DMA((2, 2))],
        3_000_000_000,
    )
    q_theirs, k_theirs = swap_core(q_share), swap_core(k_share)

    def paired(d, source, theirs):
        mine = lax.dot_general(
            cols(source), d, (((0,), (0,)), ((), ())), preferred_element_type=F32
        )
        return (mine + theirs.astype(F32)).astype(BF16)

    up_sum = paired(d_values, tok, up_theirs)
    after = along_ctx(d_prev[:1], -1)
    q_sum, k_sum = paired(d_query, tok, q_theirs), paired(d_prev, tok_prev, k_theirs)
    pair_sum = jnp.concatenate([q_sum, k_sum, up_sum], 1)
    pair_sum, after = lax.optimization_barrier((pair_sum, after))
    exchanged = lax.all_to_all(
        pair_sum.reshape(64, -1, pair_sum.shape[1]), ("xl", "dp", "z", "xh"), 0, 0, tiled=True
    )
    summed = lax.all_to_all(sum_ranks(exchanged, 32), ("dp", "z", "xh"), 0, 0, tiled=True)

    d_key = jnp.concatenate([d_prev[1:], after], 0)
    (grad_tokens,) = call(
        tokens_kernel,
        (place,),
        (d_query, d_key, d_values, w_query, q1, q2, q3, w_key, k1, k2, k3,
         *up, *u1, u2_low, u2_high, *u3),
        (),
        ((flat, BF16),),
        [buf(flat, BF16), buf(flat, BF16), buf(wide, BF16), buf(square, BF16), buf(square, BF16),
         buf(tall, BF16), DMA((3,)), DMA((4,)), DMA((4,)), DMA((8,))],
        5_000_000_000,
    )
    grads = widen(summed, (width, width, hidden))
    return (dechunked[None], grad_tokens[None], *grads)


def solution(mesh):
    split = jax.sharding.Mesh(
        mesh.devices.reshape(4, 2, 2, 4, 2), ("dp", "xl", "core", "z", "xh")
    )
    rows = P(("xl", "core"), None)
    data = P(("dp", "xl", "core"), CTX, None)
    return jax.shard_map(
        per_device,
        mesh=split,
        in_specs=(data, P(("dp", "xl", "core"), CTX), P(), rows, rows, rows, data),
        out_specs=(data, data, rows, rows, rows),
        check_vma=False,
    )
```

```python
import functools

import jax
import jax.numpy as jnp
from jax import lax
from jax.experimental import pallas as pl
from jax.experimental.pallas import tpu as pltpu
from jax.sharding import PartitionSpec as P

SPAN = 128
LANES = 128
epsilon = 1e-06
CTX = ("z", "xh")
RANGES = 8
HIGHEST = lax.Precision.HIGHEST
F32 = jnp.float32
BF16 = jnp.bfloat16


def along_x(a, by):
    pairs = []
    for xl in range(2):
        for xh in range(2):
            x = (xh * 2 + xl + by) % 4
            pairs.append((xl * 2 + xh, (x % 2) * 2 + x // 2))
    return lax.ppermute(a, ("xl", "xh"), pairs)


def swap_core(a):
    return lax.ppermute(a, "core", [(0, 1), (1, 0)])


def along_ctx(a, by):
    return lax.ppermute(
        a, CTX, [(i, i + by) for i in range(RANGES) if 0 <= i + by < RANGES]
    )


def mxu(a, b):
    return jnp.dot(a, b, preferred_element_type=F32)


def halves(a):
    high = a.astype(BF16)
    return high, (a - high.astype(F32)).astype(BF16)


def ids(shape, dim):
    return lax.broadcasted_iota(jnp.int32, shape, dim)


def head_cols(h):
    return slice(h * LANES, (h + 1) * LANES)


def span(n):
    return pl.ds(pl.multiple_of(n * SPAN, SPAN), SPAN)


def fetch_panel(place, pieces, whole, sems):
    rows = whole.shape[0] // 4
    copies = []
    for j, piece in enumerate(pieces):
        at = pl.multiple_of((place[0] ^ (j // (len(pieces) // 4))) * rows, rows)
        part = piece.shape[0]
        start = at + (j % (len(pieces) // 4)) * part
        copies.append(
            pltpu.make_async_copy(
                piece, whole.at[pl.ds(pl.multiple_of(start, part), part), :], sems.at[j]
            )
        )
    return copies


def block_copy(source, target, sems, n):
    return pltpu.make_async_copy(source.at[span(n), :], target.at[span(n), :], sems.at[n])


def whole_copy(source, target, sem):
    return pltpu.make_async_copy(source, target, sem)


def rates_kernel(
    place, bounds, decay, tok, tok_prev, cot, q0, q1, q2, q3, k0, k1, k2, k3,
    queries, keys, adjoint, mix_out, keep_out, stats_out, outs, carry,
    wq, wk, q_sems, k_sems,
):
    hidden = adjoint.shape[1]
    heads = hidden // LANES
    blocks = adjoint.shape[0] // SPAN
    load_q = fetch_panel(place, (q0, q1, q2, q3), wq, q_sems)
    load_k = fetch_panel(place, (k0, k1, k2, k3), wk, k_sems)
    for c in load_q + load_k:
        c.start()
    carry[0:1, :] = jnp.zeros((1, hidden), F32)
    carry[1:2, :] = jnp.ones((1, hidden), F32)
    for c in load_q:
        c.wait()
    queries[...] = mxu(tok[...], wq[...])
    for c in load_k:
        c.wait()
    keys[...] = mxu(tok_prev[...], wk[...])

    @pl.loop(0, blocks)
    def _(step):
        n = blocks - 1 - step
        rows = span(n)
        q, k = queries[rows, :], keys[rows, :]
        iq = lax.rsqrt(jnp.sum(q * q, -1, keepdims=True) + epsilon)
        ik = lax.rsqrt(jnp.sum(k * k, -1, keepdims=True) + epsilon)
        cosine = jnp.sum(q * k, -1, keepdims=True) * iq * ik
        lane = ids((SPAN, LANES), 1)
        sub = ids((SPAN, LANES), 0)
        first = jnp.logical_and(place[1] + place[2] == 0, n == 0)
        opening = jnp.logical_and(first, ids((SPAN, 1), 0) == 0)
        prob = jnp.where(opening, 1.0, 0.5 * (1.0 - cosine))
        marked = jnp.where(opening, 1.0, bounds[rows, :])
        mix = (marked * prob) * decay[...]
        logs = jnp.log(1.0 - mix)
        lower = (sub >= lane).astype(F32)
        keep = jnp.dot(lower, logs, precision=HIGHEST, preferred_element_type=F32)
        keep_rows = keep.T
        active = jnp.where(opening, 0.0, marked)
        stats = jnp.where(
            lane == 0, iq, jnp.where(lane == 1, ik, jnp.where(lane == 2, cosine, active))
        )
        mix_out[rows, :] = mix
        keep_out[rows, :] = keep
        stats_out[rows, :] = stats
        outs[pl.ds(n, 1), :] = carry[0:1, :]
        total = jnp.exp(keep[SPAN - 1 : SPAN, :])
        upper = sub <= lane
        for h in range(heads):
            cols = head_cols(h)
            gap = keep_rows[h : h + 1, :] - keep[:, h : h + 1]
            band = jnp.where(upper, jnp.exp(jnp.where(upper, gap, 0.0)), 0.0)
            high, low = halves(band)
            g = cot[rows, cols]
            local = mxu(high, g) + mxu(low, g)
            adjoint[rows, cols] = local
            d = total[:, h : h + 1]
            carry[0:1, cols] = d * carry[0:1, cols] + (1.0 - mix[0:1, h : h + 1]) * local[0:1, :]
            carry[1:2, cols] = d * carry[1:2, cols]


def states_kernel(
    place, mix_ref, keep_ref, tok, b_carry, u0, u1, u2, u3, u4, u5, u6, u7,
    values, states, ins, message,
    wu, carry, u_sems,
):
    hidden = values.shape[1]
    heads = hidden // LANES
    blocks = values.shape[0] // SPAN
    pieces = (u0, u1, u2, u3, u4, u5, u6, u7)
    parts = (slice(0, hidden // 2), slice(hidden // 2, hidden))
    loads = [
        fetch_panel(place, [u.at[:, part] for u in pieces], wu.at[:, part], u_sems.at[i])
        for i, part in enumerate(parts)
    ]
    for c in loads[0] + loads[1]:
        c.start()
    carry[...] = jnp.zeros_like(carry)
    message[0:2, :] = b_carry[...]
    for i, part in enumerate(parts):
        for c in loads[i]:
            c.wait()
        values[:, part] = mxu(tok[...], wu[:, part])

    @pl.loop(0, blocks)
    def _(n):
        rows = span(n)
        mix, keep = mix_ref[rows, :], keep_ref[rows, :]
        keep_rows = keep.T
        lower = ids((SPAN, LANES), 0) >= ids((SPAN, LANES), 1)
        ins[pl.ds(n, 1), :] = carry[0:1, :]
        total = jnp.exp(keep[SPAN - 1 : SPAN, :])
        for h in range(heads):
            cols = head_cols(h)
            gap = keep[:, h : h + 1] - keep_rows[h : h + 1, :]
            band = jnp.where(lower, jnp.exp(jnp.where(lower, gap, 0.0)), 0.0)
            high, low = halves(band)
            added, rest = halves(mix[:, h : h + 1] * values[rows, cols])
            local = mxu(high, added) + mxu(low, added) + mxu(high, rest)
            states[rows, cols] = local
            carry[0:1, cols] = total[:, h : h + 1] * carry[0:1, cols] + local[SPAN - 1 : SPAN, :]

    message[2:3, :] = carry[...]


def chain(own, message, incoming, row):
    return jnp.where(own, message[1:2, :] * incoming + message[row : row + 1, :], incoming)


def pair_kernel(place, message, other, pair):
    low = jnp.where(place[2] == 0, message[...], other[...])
    high = jnp.where(place[2] == 0, other[...], message[...])
    pair[0:1, :] = low[1:2] * high[0:1] + low[0:1]
    pair[1:2, :] = low[1:2] * high[1:2]
    pair[2:3, :] = high[1:2] * low[2:3] + high[2:3]


def adjoint_in(place, other, after):
    incoming = jnp.zeros((1, other.shape[1]), F32)
    for d in (3, 2, 1):
        incoming = chain(place[1] + d <= 3, after[d - 1], incoming, 0)
    return chain(place[2] == 0, other, incoming, 0)


def state_in(place, other, after):
    incoming = jnp.zeros((1, other.shape[1]), F32)
    for d in (3, 2, 1):
        incoming = chain(place[1] - d >= 0, after[3 - d], incoming, 2)
    return chain(place[2] == 1, other, incoming, 2)


def side_columns(core, source, target, sems):
    rows = target.shape[1] // 2
    copies = []
    for b in range(2):
        start = pl.multiple_of((2 * b + core) * rows, rows)
        copies.append(
            pltpu.make_async_copy(
                source.at[:, pl.ds(start, rows)],
                target.at[:, b * rows : (b + 1) * rows],
                sems.at[b],
            )
        )
    return copies


def shares(lhs, d, share, share_out, sems):
    step = 512
    saves = []
    for i in range(d.shape[1] // step):
        part = slice(i * step, (i + 1) * step)
        share[:, part] = lax.dot_general(
            lhs[...], d[:, part], (((0,), (0,)), ((), ())), preferred_element_type=F32
        ).astype(BF16)
        saves.append(whole_copy(share.at[:, part], share_out.at[:, part], sems.at[i]))
        saves[i].start()
    return saves


def adjoint_kernel(
    place, outs, mix_ref, keep_ref, other, next1, next2, next3, local, theirs_in,
    d_values, tails, share_out, theirs, share, s_sems, t_sems,
):
    heads = local.shape[1] // LANES
    blocks = local.shape[0] // SPAN
    sides = side_columns(1 - place[0] % 2, theirs_in, theirs, t_sems)
    for c in sides:
        c.start()
    incoming = adjoint_in(place, other, (next1, next2, next3))

    def block(step, after):
        n = blocks - 1 - step
        rows = span(n)
        mix, keep = mix_ref[rows, :], keep_ref[rows, :]
        last = keep[SPAN - 1 : SPAN, :]
        fade = jnp.exp(last - keep)
        reach = jnp.exp(after)
        back = outs[pl.ds(n, 1), :]
        ends = []
        for h in range(heads):
            cols = head_cols(h)
            tail = back[:, cols] + reach[:, h : h + 1] * incoming[:, cols]
            ends.append(tail)
            full = local[rows, cols] + fade[:, h : h + 1] * tail
            d_values[rows, cols] = (mix[:, h : h + 1] * full).astype(BF16)
        tails[pl.ds(n, 1), :] = jnp.concatenate(ends, 1)
        return after + last

    lax.fori_loop(0, blocks, block, jnp.zeros((1, LANES), F32))
    for c in sides:
        c.wait()
    saves = shares(theirs, d_values, share, share_out, s_sems)
    for c in saves:
        c.wait()


def router_kernel(
    place, ins, tails, keep_ref, stats_ref, decay, other, next1, next2, next3,
    local, values, adjoint, queries, keys, now_in, prev_in,
    d_query, d_prev, dechunked_out, q_share_out, k_share_out,
    dechunked, now, prev, q_share, k_share, d_sems, qs_sems, ks_sems, t_sems,
):
    heads = values.shape[1] // LANES
    blocks = values.shape[0] // SPAN
    sides = side_columns(1 - place[0] % 2, now_in, now, t_sems.at[0])
    sides += side_columns(1 - place[0] % 2, prev_in, prev, t_sems.at[1])
    for c in sides:
        c.start()
    incoming = state_in(place, other, (next1, next2, next3))

    def block(n, before):
        rows = span(n)
        keep = keep_ref[rows, :]
        fade = jnp.exp(keep)
        last = keep[SPAN - 1 : SPAN, :]
        fade_back = jnp.exp(last - keep)
        reach = jnp.exp(before)
        start = ins[pl.ds(n, 1), :]
        tail = tails[pl.ds(n, 1), :]
        top = ids((SPAN, LANES), 0) == 0
        total = jnp.zeros((SPAN, LANES), F32)
        for h in range(heads):
            cols = head_cols(h)
            base = start[:, cols] + reach[:, h : h + 1] * incoming[:, cols]
            state = local[rows, cols] + fade[:, h : h + 1] * base
            dechunked[rows, cols] = state.astype(BF16)
            earlier = jnp.where(top, base, pltpu.roll(state, 1, 0))
            full = adjoint[rows, cols] + fade_back[:, h : h + 1] * tail[:, cols]
            total = total + (decay[:, h : h + 1] * full) * (values[rows, cols] - earlier)
        stats = stats_ref[rows, :]
        iq, ik, cosine, active = (stats[:, i : i + 1] for i in range(4))
        d_cos = -0.5 * (active * jnp.sum(total, -1, keepdims=True))
        both = d_cos * (iq * ik)
        over_q, over_k = d_cos * (cosine * iq * iq), d_cos * (cosine * ik * ik)
        q, k = queries[rows, :], keys[rows, :]
        d_query[rows, :] = (k * both - over_q * q).astype(BF16)
        d_prev[rows, :] = (q * both - over_k * k).astype(BF16)
        block_copy(dechunked, dechunked_out, d_sems, n).start()
        return before + last

    lax.fori_loop(0, blocks, block, jnp.zeros((1, LANES), F32))
    for c in sides:
        c.wait()
    out = shares(now, d_query, q_share, q_share_out, qs_sems)
    out += shares(prev, d_prev, k_share, k_share_out, ks_sems)
    for c in out:
        c.wait()
    for n in range(blocks):
        block_copy(dechunked, dechunked_out, d_sems, n).wait()


def up_sum_kernel(place, d_values, theirs, tok_in, out, tok, sems):
    sides = side_columns(place[0] % 2, tok_in, tok, sems)
    for c in sides:
        c.start()
    for c in sides:
        c.wait()
    at = out.shape[1] - d_values.shape[1]
    add_share(tok, d_values, theirs, out, at)


def route_sum_kernel(
    place, d_query, d_prev, q_theirs, k_theirs, partial, now_in, prev_in, out, now, prev, sems,
):
    sides = side_columns(place[0] % 2, now_in, now, sems.at[0])
    sides += side_columns(place[0] % 2, prev_in, prev, sems.at[1])
    for c in sides:
        c.start()
    for c in sides:
        c.wait()
    add_share(now, d_query, q_theirs, out, 0)
    add_share(prev, d_prev, k_theirs, out, d_query.shape[1])


def add_share(lhs, d, theirs, out, at):
    step = 512
    for i in range(d.shape[1] // step):
        part = slice(i * step, (i + 1) * step)
        mine = lax.dot_general(
            lhs[...], d[:, part], (((0,), (0,)), ((), ())), preferred_element_type=F32
        )
        total = mine + theirs[:, part].astype(F32)
        out[:, at + i * step : at + (i + 1) * step] = total.astype(BF16)


def tokens_kernel(place, d_query_in, d_key_in, d_values_in, *refs):
    pieces, out = refs[:16], refs[16]
    d_query, d_key, d_values, wq, wk, wu, d_sems, q_sems, k_sems, u_sems = refs[17:]
    loads = [
        whole_copy(source, target, d_sems.at[i])
        for i, (source, target) in enumerate(
            ((d_query_in, d_query), (d_key_in, d_key), (d_values_in, d_values))
        )
    ]
    loads += fetch_panel(place, pieces[:4], wq, q_sems)
    loads += fetch_panel(place, pieces[4:8], wk, k_sems)
    loads += fetch_panel(place, pieces[8:], wu, u_sems)
    for c in loads:
        c.start()
    for c in loads:
        c.wait()
    dims = (((1,), (1,)), ((), ()))
    rows = wq.shape[0] // 4
    for j in range(4):
        part = slice(j * rows, (j + 1) * rows)
        terms = [
            lax.dot_general(d[...], w[part, :], dims, preferred_element_type=F32)
            for d, w in ((d_query, wq), (d_key, wk), (d_values, wu))
        ]
        out[:, part] = (terms[0] + terms[1] + terms[2]).astype(BF16)


def sum_kernel(parts, out):
    step = 512
    for i in range(out.shape[2] // step):
        cols = slice(i * step, (i + 1) * step)
        acc = parts[0, :, cols].astype(F32)
        for j in range(1, parts.shape[0]):
            acc = acc + parts[j, :, cols].astype(F32)
        rounded = acc.astype(BF16)
        for j in range(out.shape[0]):
            out[j, :, cols] = rounded


def sum_ranks(exchanged, copies):
    _, depth, width = exchanged.shape
    return pl.pallas_call(
        sum_kernel,
        out_shape=jax.ShapeDtypeStruct((copies, depth, width), BF16),
        in_specs=[VMEM],
        out_specs=VMEM,
        compiler_params=pltpu.CompilerParams(vmem_limit_bytes=16 << 20),
    )(exchanged)


def widen_kernel(parts, *refs):
    outs, bufs, sems = refs[:3], refs[3:6], refs[6]
    ranks, depth, _ = parts.shape
    chunks = 4
    group = ranks // chunks
    copies = []
    for i in range(chunks):
        start = 0
        for o, (out, buf) in enumerate(zip(outs, bufs)):
            width = out.shape[1]
            for j in range(i * group, (i + 1) * group):
                buf[j * depth : (j + 1) * depth, :] = parts[j, :, start : start + width].astype(F32)
            rows = pl.ds(i * group * depth, group * depth)
            copies.append(
                pltpu.make_async_copy(buf.at[rows, :], out.at[rows, :], sems.at[o * chunks + i])
            )
            copies[-1].start()
            start += width
    for c in copies:
        c.wait()


def widen(summed, widths):
    ranks, depth, _ = summed.shape
    shapes = [(ranks * depth, w) for w in widths]
    return pl.pallas_call(
        widen_kernel,
        out_shape=[jax.ShapeDtypeStruct(s, F32) for s in shapes],
        in_specs=[VMEM],
        out_specs=[HBM] * len(widths),
        scratch_shapes=[pltpu.VMEM(s, F32) for s in shapes] + [DMA((12,))],
        compiler_params=pltpu.CompilerParams(vmem_limit_bytes=16 << 20),
    )(summed)


SMEM = pl.BlockSpec(memory_space=pltpu.SMEM)
VMEM = pl.BlockSpec(memory_space=pltpu.VMEM)
HBM = pl.BlockSpec(memory_space=pltpu.HBM)
DMA = pltpu.SemaphoreType.DMA
VMEM_LIMIT = 62 << 20


def in_hbm(a):
    return pltpu.with_memory_space_constraint(a, pltpu.HBM)


def call(
    body, place, vmem_args, hbm_args, vmem_outs, hbm_outs, scratch, flops, limit, aliases=None
):
    return pl.pallas_call(
        body,
        out_shape=[jax.ShapeDtypeStruct(s, t) for s, t in vmem_outs]
        + [pltpu.HBM(s, t) for s, t in hbm_outs],
        in_specs=[SMEM] + [VMEM] * len(vmem_args) + [HBM] * len(hbm_args),
        out_specs=[VMEM] * len(vmem_outs) + [HBM] * len(hbm_outs),
        scratch_shapes=scratch,
        input_output_aliases=aliases or {},
        cost_estimate=pl.CostEstimate(flops=flops, bytes_accessed=1 << 20, transcendentals=0),
        compiler_params=pltpu.CompilerParams(vmem_limit_bytes=limit << 20),
    )(place, *vmem_args, *[in_hbm(a) for a in hbm_args])


def per_device(tokens, bounds, decay_rates, w_query, w_key, w_up, grad_out):
    _, length, width = tokens.shape
    hidden = w_up.shape[1]
    heads = decay_rates.shape[0]
    rows = w_query.shape[0]
    blocks = length // SPAN
    tok, cot = tokens[0], grad_out[0]
    core, high = lax.axis_index("core"), lax.axis_index("xh")
    place = jnp.stack(
        [lax.axis_index("xl") * 2 + core, lax.axis_index("z"), high]
    ).astype(jnp.int32)

    q2, k2 = along_x(w_query, -1), along_x(w_key, 1)
    q1, k1 = swap_core(w_query), swap_core(w_key)
    before = along_ctx(tok[-1:], 1)
    tok_prev = jnp.concatenate([before, tok[:-1]], 0)
    half = rows // 2
    up = (w_up[:half], w_up[half:])
    up_low, up_high, q2 = lax.optimization_barrier((*up, q2))
    q3, k3 = swap_core(q2), swap_core(k2)
    u2 = (along_x(up_low, -1), along_x(up_high, 1))
    u1 = tuple(swap_core(u) for u in up)

    marks = bounds[0].astype(F32)[:, None]
    decay = jnp.pad(decay_rates, (0, LANES - heads))[None]
    flat, wide, narrow = (length, width), (length, hidden), (length, LANES)
    square, tall, per_block = (width, width), (width, hidden), (blocks, hidden)
    buf = pltpu.VMEM
    queries, keys, local_adjoint, mix, keep, stats, outs, b_carry = call(
        rates_kernel, place,
        (marks, decay, tok, tok_prev, cot),
        (w_query, q1, q2, q3, w_key, k1, k2, k3),
        ((flat, F32), (flat, F32), (wide, F32), (narrow, F32), (narrow, F32), (narrow, F32),
         (per_block, F32), ((2, hidden), F32)),
        (),
        [buf(square, BF16), buf(square, BF16), DMA((4,)), DMA((4,))],
        8_000_000_000, 16,
    )
    u2_low, u2_high, keep_late = lax.optimization_barrier((*u2, keep))
    u3 = (swap_core(u2_low), swap_core(u2_high))
    values, local_states, ins, message = call(
        states_kernel, place,
        (mix, keep_late, tok, b_carry),
        (*up, *u1, u2_low, u2_high, *u3),
        ((wide, F32), (wide, F32), (per_block, F32), ((3, hidden), F32)),
        (),
        [buf(tall, BF16), buf((1, hidden), F32), DMA((2, 8))],
        8_000_000_000, 16,
    )
    other = lax.ppermute(message, "xh", [(0, 1), (1, 0)])
    (pair,) = call(
        pair_kernel, place, (message, other), (), (((3, hidden), F32),), (), [], 1_000_000, 4
    )
    messages = [other] + [
        lax.ppermute(pair, "z", [(i, (i - d) % 4) for i in range(4)]) for d in (1, 2, 3)
    ]

    side, half_flat, half_wide = (length, 2 * rows), (2 * rows, width), (2 * rows, hidden)
    d_values, tails, up_share = call(
        adjoint_kernel, place,
        (outs, mix, keep, *messages, local_adjoint),
        (tok,),
        ((wide, BF16), (per_block, F32)),
        ((half_wide, BF16),),
        [buf(side, BF16), buf(half_wide, BF16), DMA((4,)), DMA((2,))],
        3_000_000_000, 16,
    )
    up_theirs = swap_core(up_share)
    d_query, d_prev, dechunked, q_share, k_share = call(
        router_kernel, place,
        (ins, tails, keep, stats, decay, *messages, local_states, values, local_adjoint,
         queries, keys),
        (tok, tok_prev),
        ((flat, BF16), (flat, BF16)),
        ((wide, BF16), (half_flat, BF16), (half_flat, BF16)),
        [buf(wide, BF16), buf(side, BF16), buf(side, BF16), buf(half_flat, BF16),
         buf(half_flat, BF16), DMA((blocks,)), DMA((2,)), DMA((2,)), DMA((2, 2))],
        3_000_000_000, 16,
    )
    q_theirs, k_theirs = swap_core(q_share), swap_core(k_share)

    full = (2 * rows, 2 * width + hidden)
    (partial,) = call(
        up_sum_kernel, place,
        (d_values, up_theirs), (tok,), ((full, BF16),), (),
        [buf(side, BF16), DMA((2,))], 1_500_000_000, 8,
    )
    after = along_ctx(d_prev[:1], -1)
    (pair_sum,) = call(
        route_sum_kernel, place,
        (d_query, d_prev, q_theirs, k_theirs, partial), (tok, tok_prev), ((full, BF16),), (),
        [buf(side, BF16), buf(side, BF16), DMA((2, 2))], 1_500_000_000, 8, {5: 0},
    )
    pair_sum, after = lax.optimization_barrier((pair_sum, after))
    exchanged = lax.all_to_all(
        pair_sum.reshape(64, -1, pair_sum.shape[1]), ("xl", "dp", "z", "xh"), 0, 0, tiled=True
    )
    summed = lax.all_to_all(sum_ranks(exchanged, 32), ("dp", "z", "xh"), 0, 0, tiled=True)

    d_key = jnp.concatenate([d_prev[1:], after], 0)
    (grad_tokens,) = call(
        tokens_kernel, place,
        (),
        (d_query, d_key, d_values, w_query, q1, q2, q3, w_key, k1, k2, k3,
         *up, *u1, u2_low, u2_high, *u3),
        ((flat, BF16),),
        (),
        [buf(flat, BF16), buf(flat, BF16), buf(wide, BF16), buf(square, BF16), buf(square, BF16),
         buf(tall, BF16), DMA((3,)), DMA((4,)), DMA((4,)), DMA((8,))],
        5_000_000_000, 60,
    )
    grads = widen(summed, (width, width, hidden))
    return (dechunked[None], grad_tokens[None], *grads)


def solution(mesh):
    split = jax.sharding.Mesh(
        mesh.devices.reshape(4, 2, 2, 4, 2), ("dp", "xl", "core", "z", "xh")
    )
    rows = P(("xl", "core"), None)
    data = P(("dp", "xl", "core"), CTX, None)
    return jax.shard_map(
        per_device,
        mesh=split,
        in_specs=(data, P(("dp", "xl", "core"), CTX), P(), rows, rows, rows, data),
        out_specs=(data, data, rows, rows, rows),
        check_vma=False,
    )
```

```python
import functools

import jax
import jax.numpy as jnp
from jax import lax
from jax.experimental import pallas as pl
from jax.experimental.pallas import tpu as pltpu
from jax.sharding import PartitionSpec as P

SPAN = 128
LANES = 128
epsilon = 1e-06
CTX = ("z", "xh")
RANGES = 8
HIGHEST = lax.Precision.HIGHEST
F32 = jnp.float32
BF16 = jnp.bfloat16


def along_x(a, by):
    pairs = []
    for xl in range(2):
        for xh in range(2):
            x = (xh * 2 + xl + by) % 4
            pairs.append((xl * 2 + xh, (x % 2) * 2 + x // 2))
    return lax.ppermute(a, ("xl", "xh"), pairs)


def swap_core(a):
    return lax.ppermute(a, "core", [(0, 1), (1, 0)])


def along_ctx(a, by):
    return lax.ppermute(
        a, CTX, [(i, i + by) for i in range(RANGES) if 0 <= i + by < RANGES]
    )


def mxu(a, b):
    return jnp.dot(a, b, preferred_element_type=F32)


def halves(a):
    high = a.astype(BF16)
    return high, (a - high.astype(F32)).astype(BF16)


def ids(shape, dim):
    return lax.broadcasted_iota(jnp.int32, shape, dim)


def head_cols(h):
    return slice(h * LANES, (h + 1) * LANES)


def span(n):
    return pl.ds(pl.multiple_of(n * SPAN, SPAN), SPAN)


def fetch_panel(place, pieces, whole, sems):
    core = place[0] % 2
    split = len(pieces) // 2
    rows = whole.shape[0] // 2
    copies = []
    for j, piece in enumerate(pieces):
        part = piece.shape[0]
        start = (core ^ (j // split)) * rows + (j % split) * part
        copies.append(
            pltpu.make_async_copy(
                piece, whole.at[pl.ds(pl.multiple_of(start, part), part), :], sems.at[j]
            )
        )
    return copies


def block_copy(source, target, sems, n):
    return pltpu.make_async_copy(source.at[span(n), :], target.at[span(n), :], sems.at[n])


def whole_copy(source, target, sem):
    return pltpu.make_async_copy(source, target, sem)


def panel_columns(index, depth):
    return pl.ds(pl.multiple_of(index * depth, depth), depth)


def near_kernel(
    place, tok, tok_prev, q0, q1, k0, k1, queries, keys, turned, turned_prev, wq, wk, q_sems, k_sems,
):
    loads = fetch_panel(place, (q0, q1), wq, q_sems), fetch_panel(place, (k0, k1), wk, k_sems)
    for c in loads[0] + loads[1]:
        c.start()
    cols = panel_columns(place[0] // 2, wq.shape[0])
    turned[...] = tok[...].T
    turned_prev[...] = tok_prev[...].T
    for c in loads[0]:
        c.wait()
    queries[...] = mxu(tok[:, cols], wq[...])
    for c in loads[1]:
        c.wait()
    keys[...] = mxu(tok_prev[:, cols], wk[...])


def near_values_kernel(place, tok, u0, u1, u2, u3, values, wu, sems):
    loads = fetch_panel(place, (u0, u1, u2, u3), wu, sems)
    for c in loads:
        c.start()
    for c in loads:
        c.wait()
    values[...] = mxu(tok[:, panel_columns(place[0] // 2, wu.shape[0])], wu[...])


def rates_kernel(
    place, bounds, decay, tok, tok_prev, cot, q_part, k_part, q2, q3, k2, k3,
    queries, keys, adjoint, mix_out, keep_out, stats_out, outs, carry,
    wq, wk, q_sems, k_sems,
):
    hidden = adjoint.shape[1]
    heads = hidden // LANES
    blocks = adjoint.shape[0] // SPAN
    load_q = fetch_panel(place, (q2, q3), wq, q_sems)
    load_k = fetch_panel(place, (k2, k3), wk, k_sems)
    for c in load_q + load_k:
        c.start()
    carry[0:1, :] = jnp.zeros((1, hidden), F32)
    carry[1:2, :] = jnp.ones((1, hidden), F32)
    cols = panel_columns(1 - place[0] // 2, wq.shape[0])
    for c in load_q:
        c.wait()
    queries[...] = q_part[...] + mxu(tok[:, cols], wq[...])
    for c in load_k:
        c.wait()
    keys[...] = k_part[...] + mxu(tok_prev[:, cols], wk[...])

    @pl.loop(0, blocks)
    def _(step):
        n = blocks - 1 - step
        rows = span(n)
        q, k = queries[rows, :], keys[rows, :]
        iq = lax.rsqrt(jnp.sum(q * q, -1, keepdims=True) + epsilon)
        ik = lax.rsqrt(jnp.sum(k * k, -1, keepdims=True) + epsilon)
        cosine = jnp.sum(q * k, -1, keepdims=True) * iq * ik
        lane = ids((SPAN, LANES), 1)
        sub = ids((SPAN, LANES), 0)
        first = jnp.logical_and(place[1] + place[2] == 0, n == 0)
        opening = jnp.logical_and(first, ids((SPAN, 1), 0) == 0)
        prob = jnp.where(opening, 1.0, 0.5 * (1.0 - cosine))
        marked = jnp.where(opening, 1.0, bounds[rows, :])
        mix = (marked * prob) * decay[...]
        logs = jnp.log(1.0 - mix)
        lower = (sub >= lane).astype(F32)
        keep = jnp.dot(lower, logs, precision=HIGHEST, preferred_element_type=F32)
        keep_rows = keep.T
        active = jnp.where(opening, 0.0, marked)
        stats = jnp.where(
            lane == 0, iq, jnp.where(lane == 1, ik, jnp.where(lane == 2, cosine, active))
        )
        mix_out[rows, :] = mix
        keep_out[rows, :] = keep
        stats_out[rows, :] = stats
        outs[pl.ds(n, 1), :] = carry[0:1, :]
        total = jnp.exp(keep[SPAN - 1 : SPAN, :])
        upper = sub <= lane
        for h in range(heads):
            cols = head_cols(h)
            gap = keep_rows[h : h + 1, :] - keep[:, h : h + 1]
            band = jnp.where(upper, jnp.exp(jnp.where(upper, gap, 0.0)), 0.0)
            high, low = halves(band)
            g = cot[rows, cols]
            local = mxu(high, g) + mxu(low, g)
            adjoint[rows, cols] = local
            d = total[:, h : h + 1]
            carry[0:1, cols] = d * carry[0:1, cols] + (1.0 - mix[0:1, h : h + 1]) * local[0:1, :]
            carry[1:2, cols] = d * carry[1:2, cols]


def states_kernel(
    place, mix_ref, keep_ref, tok, b_carry, v_part, u4, u5, u6, u7,
    values, states, ins, message,
    wu, carry, u_sems,
):
    hidden = values.shape[1]
    heads = hidden // LANES
    blocks = values.shape[0] // SPAN
    loads = fetch_panel(place, (u4, u5, u6, u7), wu, u_sems)
    for c in loads:
        c.start()
    carry[...] = jnp.zeros_like(carry)
    message[0:2, :] = b_carry[...]
    cols = panel_columns(1 - place[0] // 2, wu.shape[0])
    for c in loads:
        c.wait()
    values[...] = v_part[...] + mxu(tok[:, cols], wu[...])

    @pl.loop(0, blocks)
    def _(n):
        rows = span(n)
        mix, keep = mix_ref[rows, :], keep_ref[rows, :]
        keep_rows = keep.T
        lower = ids((SPAN, LANES), 0) >= ids((SPAN, LANES), 1)
        ins[pl.ds(n, 1), :] = carry[0:1, :]
        total = jnp.exp(keep[SPAN - 1 : SPAN, :])
        for h in range(heads):
            cols = head_cols(h)
            gap = keep[:, h : h + 1] - keep_rows[h : h + 1, :]
            band = jnp.where(lower, jnp.exp(jnp.where(lower, gap, 0.0)), 0.0)
            high, low = halves(band)
            added, rest = halves(mix[:, h : h + 1] * values[rows, cols])
            local = mxu(high, added) + mxu(low, added) + mxu(high, rest)
            states[rows, cols] = local
            carry[0:1, cols] = total[:, h : h + 1] * carry[0:1, cols] + local[SPAN - 1 : SPAN, :]

    message[2:3, :] = carry[...]


def chain(own, message, incoming, row):
    return jnp.where(own, message[1:2, :] * incoming + message[row : row + 1, :], incoming)


def pair_kernel(place, message, other, pair):
    low = jnp.where(place[2] == 0, message[...], other[...])
    high = jnp.where(place[2] == 0, other[...], message[...])
    pair[0:1, :] = low[1:2] * high[0:1] + low[0:1]
    pair[1:2, :] = low[1:2] * high[1:2]
    pair[2:3, :] = high[1:2] * low[2:3] + high[2:3]


def adjoint_in(place, other, after):
    incoming = jnp.zeros((1, other.shape[1]), F32)
    for d in (3, 2, 1):
        incoming = chain(place[1] + d <= 3, after[d - 1], incoming, 0)
    return chain(place[2] == 0, other, incoming, 0)


def state_in(place, other, after):
    incoming = jnp.zeros((1, other.shape[1]), F32)
    for d in (3, 2, 1):
        incoming = chain(place[1] - d >= 0, after[3 - d], incoming, 2)
    return chain(place[2] == 1, other, incoming, 2)


def side_rows(core, turned, b):
    rows = turned.shape[0] // 4
    return turned[pl.ds(pl.multiple_of((2 * b + core) * rows, rows), rows), :]


def shares(core, turned, d, share, share_out, sems):
    step = 512
    saves = []
    rows = share.shape[0] // 2
    for i in range(d.shape[1] // step):
        part = slice(i * step, (i + 1) * step)
        for b in range(2):
            share[b * rows : (b + 1) * rows, part] = mxu(
                side_rows(core, turned, b), d[:, part]
            ).astype(BF16)
        saves.append(whole_copy(share.at[:, part], share_out.at[:, part], sems.at[i]))
        saves[i].start()
    return saves


def adjoint_kernel(
    place, outs, mix_ref, keep_ref, other, next1, next2, next3, local, turned,
    d_values, tails, share_out, share, s_sems,
):
    heads = local.shape[1] // LANES
    blocks = local.shape[0] // SPAN
    incoming = adjoint_in(place, other, (next1, next2, next3))

    def block(step, after):
        n = blocks - 1 - step
        rows = span(n)
        mix, keep = mix_ref[rows, :], keep_ref[rows, :]
        last = keep[SPAN - 1 : SPAN, :]
        fade = jnp.exp(last - keep)
        reach = jnp.exp(after)
        back = outs[pl.ds(n, 1), :]
        ends = []
        for h in range(heads):
            cols = head_cols(h)
            tail = back[:, cols] + reach[:, h : h + 1] * incoming[:, cols]
            ends.append(tail)
            full = local[rows, cols] + fade[:, h : h + 1] * tail
            d_values[rows, cols] = (mix[:, h : h + 1] * full).astype(BF16)
        tails[pl.ds(n, 1), :] = jnp.concatenate(ends, 1)
        return after + last

    lax.fori_loop(0, blocks, block, jnp.zeros((1, LANES), F32))
    saves = shares(1 - place[0] % 2, turned, d_values, share, share_out, s_sems)
    for c in saves:
        c.wait()


def router_kernel(
    place, ins, tails, keep_ref, stats_ref, decay, other, next1, next2, next3,
    local, values, adjoint, queries, keys, turned, turned_prev,
    d_query, d_prev, dechunked_out, q_share_out, k_share_out,
    dechunked, q_share, k_share, d_sems, qs_sems, ks_sems,
):
    heads = values.shape[1] // LANES
    blocks = values.shape[0] // SPAN
    incoming = state_in(place, other, (next1, next2, next3))

    def block(n, before):
        rows = span(n)
        keep = keep_ref[rows, :]
        fade = jnp.exp(keep)
        last = keep[SPAN - 1 : SPAN, :]
        fade_back = jnp.exp(last - keep)
        reach = jnp.exp(before)
        start = ins[pl.ds(n, 1), :]
        tail = tails[pl.ds(n, 1), :]
        top = ids((SPAN, LANES), 0) == 0
        total = jnp.zeros((SPAN, LANES), F32)
        for h in range(heads):
            cols = head_cols(h)
            base = start[:, cols] + reach[:, h : h + 1] * incoming[:, cols]
            state = local[rows, cols] + fade[:, h : h + 1] * base
            dechunked[rows, cols] = state.astype(BF16)
            earlier = jnp.where(top, base, pltpu.roll(state, 1, 0))
            full = adjoint[rows, cols] + fade_back[:, h : h + 1] * tail[:, cols]
            total = total + (decay[:, h : h + 1] * full) * (values[rows, cols] - earlier)
        stats = stats_ref[rows, :]
        iq, ik, cosine, active = (stats[:, i : i + 1] for i in range(4))
        d_cos = -0.5 * (active * jnp.sum(total, -1, keepdims=True))
        both = d_cos * (iq * ik)
        over_q, over_k = d_cos * (cosine * iq * iq), d_cos * (cosine * ik * ik)
        q, k = queries[rows, :], keys[rows, :]
        d_query[rows, :] = (k * both - over_q * q).astype(BF16)
        d_prev[rows, :] = (q * both - over_k * k).astype(BF16)
        block_copy(dechunked, dechunked_out, d_sems, n).start()
        return before + last

    lax.fori_loop(0, blocks, block, jnp.zeros((1, LANES), F32))
    out = shares(1 - place[0] % 2, turned, d_query, q_share, q_share_out, qs_sems)
    out += shares(1 - place[0] % 2, turned_prev, d_prev, k_share, k_share_out, ks_sems)
    for c in out:
        c.wait()
    for n in range(blocks):
        block_copy(dechunked, dechunked_out, d_sems, n).wait()


def up_sum_kernel(place, d_values, theirs, turned, out):
    add_share(place, turned, d_values, theirs, out, out.shape[1] - d_values.shape[1])


def route_sum_kernel(
    place, d_query, d_prev, q_theirs, k_theirs, partial, turned, turned_prev, out
):
    add_share(place, turned, d_query, q_theirs, out, 0)
    add_share(place, turned_prev, d_prev, k_theirs, out, d_query.shape[1])


def add_share(place, turned, d, theirs, out, at):
    step = 512
    rows = theirs.shape[0] // 2
    for i in range(d.shape[1] // step):
        part = slice(i * step, (i + 1) * step)
        for b in range(2):
            half = slice(b * rows, (b + 1) * rows)
            mine = mxu(side_rows(place[0] % 2, turned, b), d[:, part])
            total = mine + theirs[half, part].astype(F32)
            out[half, at + i * step : at + (i + 1) * step] = total.astype(BF16)


def tokens_kernel(place, d_query_in, d_key_in, d_values_in, *refs):
    pieces, out = refs[:16], refs[16]
    d_query, d_key, d_values, wq, wk, wu, d_sems, q_sems, k_sems, u_sems = refs[17:]
    loads = [
        whole_copy(source, target, d_sems.at[i])
        for i, (source, target) in enumerate(
            ((d_query_in, d_query), (d_key_in, d_key), (d_values_in, d_values))
        )
    ]
    for side in range(2):
        two, four = slice(2 * side, 2 * side + 2), slice(4 * side, 4 * side + 4)
        loads += fetch_panel(place, pieces[:4][two], wq.at[side], q_sems.at[side])
        loads += fetch_panel(place, pieces[4:8][two], wk.at[side], k_sems.at[side])
        loads += fetch_panel(place, pieces[8:][four], wu.at[side], u_sems.at[side])
    for c in loads:
        c.start()
    for c in loads:
        c.wait()
    dims = (((1,), (1,)), ((), ()))
    for side in range(2):
        index = side + (1 - 2 * side) * (place[0] // 2)
        terms = [
            lax.dot_general(d[...], w[side], dims, preferred_element_type=F32)
            for d, w in ((d_query, wq), (d_key, wk), (d_values, wu))
        ]
        out[:, panel_columns(index, wq.shape[1])] = (terms[0] + terms[1] + terms[2]).astype(BF16)


def sum_kernel(parts, out):
    step = 512
    for i in range(out.shape[2] // step):
        cols = slice(i * step, (i + 1) * step)
        acc = parts[0, :, cols].astype(F32)
        for j in range(1, parts.shape[0]):
            acc = acc + parts[j, :, cols].astype(F32)
        rounded = acc.astype(BF16)
        for j in range(out.shape[0]):
            out[j, :, cols] = rounded


def sum_ranks(exchanged, copies):
    _, depth, width = exchanged.shape
    return pl.pallas_call(
        sum_kernel,
        out_shape=jax.ShapeDtypeStruct((copies, depth, width), BF16),
        in_specs=[VMEM],
        out_specs=VMEM,
        compiler_params=pltpu.CompilerParams(vmem_limit_bytes=16 << 20),
    )(exchanged)


def widen_kernel(parts, *refs):
    outs, bufs, sems = refs[:3], refs[3:6], refs[6]
    ranks, depth, _ = parts.shape
    chunks = 4
    group = ranks // chunks
    copies = []
    for i in range(chunks):
        start = 0
        for o, (out, buf) in enumerate(zip(outs, bufs)):
            width = out.shape[1]
            for j in range(i * group, (i + 1) * group):
                buf[j * depth : (j + 1) * depth, :] = parts[j, :, start : start + width].astype(F32)
            rows = pl.ds(i * group * depth, group * depth)
            copies.append(
                pltpu.make_async_copy(buf.at[rows, :], out.at[rows, :], sems.at[o * chunks + i])
            )
            copies[-1].start()
            start += width
    for c in copies:
        c.wait()


def widen(summed, widths):
    ranks, depth, _ = summed.shape
    shapes = [(ranks * depth, w) for w in widths]
    return pl.pallas_call(
        widen_kernel,
        out_shape=[jax.ShapeDtypeStruct(s, F32) for s in shapes],
        in_specs=[VMEM],
        out_specs=[HBM] * len(widths),
        scratch_shapes=[pltpu.VMEM(s, F32) for s in shapes] + [DMA((12,))],
        compiler_params=pltpu.CompilerParams(vmem_limit_bytes=16 << 20),
    )(summed)


SMEM = pl.BlockSpec(memory_space=pltpu.SMEM)
VMEM = pl.BlockSpec(memory_space=pltpu.VMEM)
HBM = pl.BlockSpec(memory_space=pltpu.HBM)
DMA = pltpu.SemaphoreType.DMA
VMEM_LIMIT = 62 << 20


def in_hbm(a):
    return pltpu.with_memory_space_constraint(a, pltpu.HBM)


def call(
    body, place, vmem_args, hbm_args, vmem_outs, hbm_outs, scratch, flops, limit, aliases=None
):
    return pl.pallas_call(
        body,
        out_shape=[jax.ShapeDtypeStruct(s, t) for s, t in vmem_outs]
        + [pltpu.HBM(s, t) for s, t in hbm_outs],
        in_specs=[SMEM] + [VMEM] * len(vmem_args) + [HBM] * len(hbm_args),
        out_specs=[VMEM] * len(vmem_outs) + [HBM] * len(hbm_outs),
        scratch_shapes=scratch,
        input_output_aliases=aliases or {},
        cost_estimate=pl.CostEstimate(flops=flops, bytes_accessed=1 << 20, transcendentals=0),
        compiler_params=pltpu.CompilerParams(vmem_limit_bytes=limit << 20),
    )(place, *vmem_args, *[in_hbm(a) for a in hbm_args])


def per_device(tokens, bounds, decay_rates, w_query, w_key, w_up, grad_out):
    _, length, width = tokens.shape
    hidden = w_up.shape[1]
    heads = decay_rates.shape[0]
    rows = w_query.shape[0]
    blocks = length // SPAN
    tok, cot = tokens[0], grad_out[0]
    core, high = lax.axis_index("core"), lax.axis_index("xh")
    place = jnp.stack(
        [lax.axis_index("xl") * 2 + core, lax.axis_index("z"), high]
    ).astype(jnp.int32)

    half = rows // 2
    up = (w_up[:half], w_up[half:])
    q2, k2 = along_x(w_query, -1), along_x(w_key, 1)
    q1, k1 = swap_core(w_query), swap_core(w_key)
    before = along_ctx(tok[-1:], 1)
    u2 = (along_x(up[0], -1), along_x(up[1], 1))
    tok_prev = jnp.concatenate([before, tok[:-1]], 0)
    up_low, up_high, q2 = lax.optimization_barrier((*up, q2))
    q3, k3 = swap_core(q2), swap_core(k2)
    u1 = (swap_core(up_low), swap_core(up_high))

    marks = bounds[0].astype(F32)[:, None]
    decay = jnp.pad(decay_rates, (0, LANES - heads))[None]
    flat, wide, narrow = (length, width), (length, hidden), (length, LANES)
    square, tall, per_block = (2 * rows, width), (2 * rows, hidden), (blocks, hidden)
    buf = pltpu.VMEM
    q_part, k_part, turned, turned_prev = call(
        near_kernel, place,
        (tok, tok_prev),
        (w_query, q1, w_key, k1),
        ((flat, F32), (flat, F32), ((width, length), BF16), ((width, length), BF16)),
        (),
        [buf(square, BF16), buf(square, BF16), DMA((2,)), DMA((2,))],
        2_000_000_000, 12,
    )
    (v_part,) = call(
        near_values_kernel, place, (tok,), (*up, *u1), ((wide, F32),), (),
        [buf(tall, BF16), DMA((4,))], 2_000_000_000, 12,
    )
    queries, keys, local_adjoint, mix, keep, stats, outs, b_carry = call(
        rates_kernel, place,
        (marks, decay, tok, tok_prev, cot, q_part, k_part),
        (q2, q3, k2, k3),
        ((flat, F32), (flat, F32), (wide, F32), (narrow, F32), (narrow, F32), (narrow, F32),
         (per_block, F32), ((2, hidden), F32)),
        (),
        [buf(square, BF16), buf(square, BF16), DMA((2,)), DMA((2,))],
        6_000_000_000, 16,
    )
    u2_low, u2_high, keep_late = lax.optimization_barrier((*u2, keep))
    u3 = (swap_core(u2_low), swap_core(u2_high))
    values, local_states, ins, message = call(
        states_kernel, place,
        (mix, keep_late, tok, b_carry, v_part),
        (u2_low, u2_high, *u3),
        ((wide, F32), (wide, F32), (per_block, F32), ((3, hidden), F32)),
        (),
        [buf(tall, BF16), buf((1, hidden), F32), DMA((4,))],
        6_000_000_000, 16,
    )
    other = lax.ppermute(message, "xh", [(0, 1), (1, 0)])
    (pair,) = call(
        pair_kernel, place, (message, other), (), (((3, hidden), F32),), (), [], 1_000_000, 4
    )
    messages = [other] + [
        lax.ppermute(pair, "z", [(i, (i - d) % 4) for i in range(4)]) for d in (1, 2, 3)
    ]

    half_flat, half_wide = (2 * rows, width), (2 * rows, hidden)
    d_values, tails, up_share = call(
        adjoint_kernel, place,
        (outs, mix, keep, *messages, local_adjoint, turned),
        (),
        ((wide, BF16), (per_block, F32)),
        ((half_wide, BF16),),
        [buf(half_wide, BF16), DMA((4,))],
        3_000_000_000, 16,
    )
    up_theirs = swap_core(up_share)
    d_query, d_prev, dechunked, q_share, k_share = call(
        router_kernel, place,
        (ins, tails, keep, stats, decay, *messages, local_states, values, local_adjoint,
         queries, keys, turned, turned_prev),
        (),
        ((flat, BF16), (flat, BF16)),
        ((wide, BF16), (half_flat, BF16), (half_flat, BF16)),
        [buf(wide, BF16), buf(half_flat, BF16), buf(half_flat, BF16), DMA((blocks,)), DMA((2,)),
         DMA((2,))],
        3_000_000_000, 16,
    )
    q_theirs, k_theirs = swap_core(q_share), swap_core(k_share)

    full = (2 * rows, 2 * width + hidden)
    (partial,) = call(
        up_sum_kernel, place,
        (d_values, up_theirs, turned), (), ((full, BF16),), (), [], 1_500_000_000, 8,
    )
    after = along_ctx(d_prev[:1], -1)
    (pair_sum,) = call(
        route_sum_kernel, place,
        (d_query, d_prev, q_theirs, k_theirs, partial, turned, turned_prev), (),
        ((full, BF16),), (), [], 1_500_000_000, 8, {5: 0},
    )
    pair_sum, after = lax.optimization_barrier((pair_sum, after))
    exchanged = lax.all_to_all(
        pair_sum.reshape(64, -1, pair_sum.shape[1]), ("xl", "dp", "z", "xh"), 0, 0, tiled=True
    )
    summed = lax.all_to_all(sum_ranks(exchanged, 32), ("dp", "z", "xh"), 0, 0, tiled=True)

    d_key = jnp.concatenate([d_prev[1:], after], 0)
    (grad_tokens,) = call(
        tokens_kernel, place,
        (),
        (d_query, d_key, d_values, w_query, q1, q2, q3, w_key, k1, k2, k3,
         *up, *u1, u2_low, u2_high, *u3),
        ((flat, BF16),),
        (),
        [buf(flat, BF16), buf(flat, BF16), buf(wide, BF16), buf((2, *square), BF16),
         buf((2, *square), BF16), buf((2, *tall), BF16), DMA((3,)), DMA((2, 2)), DMA((2, 2)),
         DMA((2, 4))],
        5_000_000_000, 60,
    )
    grads = widen(summed, (width, width, hidden))
    return (dechunked[None], grad_tokens[None], *grads)


def solution(mesh):
    split = jax.sharding.Mesh(
        mesh.devices.reshape(4, 2, 2, 4, 2), ("dp", "xl", "core", "z", "xh")
    )
    rows = P(("xl", "core"), None)
    data = P(("dp", "xl", "core"), CTX, None)
    return jax.shard_map(
        per_device,
        mesh=split,
        in_specs=(data, P(("dp", "xl", "core"), CTX), P(), rows, rows, rows, data),
        out_specs=(data, data, rows, rows, rows),
        check_vma=False,
    )
```

```python
import functools

import jax
import jax.numpy as jnp
from jax import lax
from jax.experimental import pallas as pl
from jax.experimental.pallas import tpu as pltpu
from jax.sharding import PartitionSpec as P


SPAN = 128
LANES = 128
epsilon = 1e-06
CTX = ("z", "xh")
RANGES = 8
HIGHEST = lax.Precision.HIGHEST
F32 = jnp.float32
BF16 = jnp.bfloat16


def along_x(a, by):
    pairs = []
    for xl in range(2):
        for xh in range(2):
            x = (xh * 2 + xl + by) % 4
            pairs.append((xl * 2 + xh, (x % 2) * 2 + x // 2))
    return lax.ppermute(a, ("xl", "xh"), pairs)


def swap_core(a):
    return lax.ppermute(a, "core", [(0, 1), (1, 0)])


def along_ctx(a, by):
    return lax.ppermute(
        a, CTX, [(i, i + by) for i in range(RANGES) if 0 <= i + by < RANGES]
    )


def mxu(a, b):
    return jnp.dot(a, b, preferred_element_type=F32)


def halves(a):
    high = a.astype(BF16)
    return high, (a - high.astype(F32)).astype(BF16)


def ids(shape, dim):
    return lax.broadcasted_iota(jnp.int32, shape, dim)


def head_cols(h):
    return slice(h * LANES, (h + 1) * LANES)


def span(n):
    return pl.ds(pl.multiple_of(n * SPAN, SPAN), SPAN)


def fetch_panel(place, pieces, whole, sems):
    core = place[0] % 2
    split = len(pieces) // 2
    rows = whole.shape[0] // 2
    copies = []
    for j, piece in enumerate(pieces):
        part = piece.shape[0]
        start = (core ^ (j // split)) * rows + (j % split) * part
        copies.append(
            pltpu.make_async_copy(
                piece, whole.at[pl.ds(pl.multiple_of(start, part), part), :], sems.at[j]
            )
        )
    return copies


def block_copy(source, target, sems, n):
    return pltpu.make_async_copy(source.at[span(n), :], target.at[span(n), :], sems.at[n])


def whole_copy(source, target, sem):
    return pltpu.make_async_copy(source, target, sem)


def panel_columns(index, depth):
    return pl.ds(pl.multiple_of(index * depth, depth), depth)


def near_kernel(place, tok, q0, q1, queries, turned, wq, q_sems):
    loads = fetch_panel(place, (q0, q1), wq, q_sems)
    for c in loads:
        c.start()
    turned[...] = tok[...].T
    for c in loads:
        c.wait()
    queries[...] = mxu(tok[:, panel_columns(place[0] // 2, wq.shape[0])], wq[...])


def near_values_kernel(
    place, tok, tok_prev, u0, u1, u2, u3, values, turned_prev, wu, sems
):
    loads = fetch_panel(place, (u0, u1, u2, u3), wu, sems)
    for c in loads:
        c.start()
    turned_prev[...] = tok_prev[...].T
    for c in loads:
        c.wait()
    values[...] = mxu(tok[:, panel_columns(place[0] // 2, wu.shape[0])], wu[...])


def rates_kernel(
    place, bounds, decay, tok, tok_prev, cot, q_part, q2, q3, k0, k1, k2, k3,
    queries, keys, adjoint, mix_out, keep_out, stats_out, outs, carry,
    wq, wk, q_sems, k_sems,
):
    hidden = adjoint.shape[1]
    heads = hidden // LANES
    blocks = adjoint.shape[0] // SPAN
    load_q = fetch_panel(place, (q2, q3), wq, q_sems)
    side, depth = place[0] // 2, wq.shape[0]
    load_k = []
    for i, pieces in enumerate(((k0, k1), (k2, k3))):
        rows = panel_columns(side + i * (1 - 2 * side), depth)
        load_k += fetch_panel(place, pieces, wk.at[rows, :], k_sems.at[i])
    for c in load_q + load_k:
        c.start()
    carry[0:1, :] = jnp.zeros((1, hidden), F32)
    carry[1:2, :] = jnp.ones((1, hidden), F32)
    cols = panel_columns(1 - side, depth)
    for c in load_q:
        c.wait()
    queries[...] = q_part[...] + mxu(tok[:, cols], wq[...])
    for c in load_k:
        c.wait()
    keys[...] = mxu(tok_prev[...], wk[...])

    @pl.loop(0, blocks)
    def _(step):
        n = blocks - 1 - step
        rows = span(n)
        q, k = queries[rows, :], keys[rows, :]
        iq = lax.rsqrt(jnp.sum(q * q, -1, keepdims=True) + epsilon)
        ik = lax.rsqrt(jnp.sum(k * k, -1, keepdims=True) + epsilon)
        cosine = jnp.sum(q * k, -1, keepdims=True) * iq * ik
        lane = ids((SPAN, LANES), 1)
        sub = ids((SPAN, LANES), 0)
        first = jnp.logical_and(place[1] + place[2] == 0, n == 0)
        opening = jnp.logical_and(first, ids((SPAN, 1), 0) == 0)
        prob = jnp.where(opening, 1.0, 0.5 * (1.0 - cosine))
        marks = jnp.broadcast_to(bounds[:, rows].astype(F32), (SPAN, SPAN)).T[:, 0:1]
        marked = jnp.where(opening, 1.0, marks)
        mix = (marked * prob) * decay[...]
        logs = jnp.log(1.0 - mix)
        lower = (sub >= lane).astype(F32)
        keep = jnp.dot(lower, logs, precision=HIGHEST, preferred_element_type=F32)
        keep_rows = keep.T
        active = jnp.where(opening, 0.0, marked)
        stats = jnp.where(
            lane == 0, iq, jnp.where(lane == 1, ik, jnp.where(lane == 2, cosine, active))
        )
        mix_out[rows, :] = mix
        keep_out[rows, :] = keep
        stats_out[rows, :] = stats
        outs[pl.ds(n, 1), :] = carry[0:1, :]
        total = jnp.exp(keep[SPAN - 1 : SPAN, :])
        upper = sub <= lane
        for h in range(heads):
            cols = head_cols(h)
            gap = keep_rows[h : h + 1, :] - keep[:, h : h + 1]
            band = jnp.where(upper, jnp.exp(jnp.where(upper, gap, 0.0)), 0.0)
            local = mxu(band.astype(BF16), cot[rows, cols])
            adjoint[rows, cols] = local
            d = total[:, h : h + 1]
            carry[0:1, cols] = d * carry[0:1, cols] + (1.0 - mix[0:1, h : h + 1]) * local[0:1, :]
            carry[1:2, cols] = d * carry[1:2, cols]


def states_kernel(
    place, mix_ref, keep_ref, tok, b_carry, v_part, u4, u5, u6, u7,
    values, states, ins, message,
    wu, carry, u_sems,
):
    hidden = values.shape[1]
    heads = hidden // LANES
    blocks = values.shape[0] // SPAN
    loads = fetch_panel(place, (u4, u5, u6, u7), wu, u_sems)
    for c in loads:
        c.start()
    carry[...] = jnp.zeros_like(carry)
    message[0:2, :] = b_carry[...]
    cols = panel_columns(1 - place[0] // 2, wu.shape[0])
    for c in loads:
        c.wait()
    values[...] = v_part[...] + mxu(tok[:, cols], wu[...])

    @pl.loop(0, blocks)
    def _(n):
        rows = span(n)
        mix, keep = mix_ref[rows, :], keep_ref[rows, :]
        keep_rows = keep.T
        lower = ids((SPAN, LANES), 0) >= ids((SPAN, LANES), 1)
        ins[pl.ds(n, 1), :] = carry[0:1, :]
        total = jnp.exp(keep[SPAN - 1 : SPAN, :])
        for h in range(heads):
            cols = head_cols(h)
            gap = keep[:, h : h + 1] - keep_rows[h : h + 1, :]
            band = jnp.where(lower, jnp.exp(jnp.where(lower, gap, 0.0)), 0.0)
            band = band.astype(BF16)
            added, rest = halves(mix[:, h : h + 1] * values[rows, cols])
            local = mxu(band, added) + mxu(band, rest)
            states[rows, cols] = local
            carry[0:1, cols] = total[:, h : h + 1] * carry[0:1, cols] + local[SPAN - 1 : SPAN, :]

    message[2:3, :] = carry[...]


def chain(own, message, incoming, row):
    return jnp.where(own, message[1:2, :] * incoming + message[row : row + 1, :], incoming)


def pair_kernel(place, message, other, pair):
    low = jnp.where(place[2] == 0, message[...], other[...])
    high = jnp.where(place[2] == 0, other[...], message[...])
    pair[0:1, :] = low[1:2] * high[0:1] + low[0:1]
    pair[1:2, :] = low[1:2] * high[1:2]
    pair[2:3, :] = high[1:2] * low[2:3] + high[2:3]


def adjoint_in(place, other, after):
    incoming = jnp.zeros((1, other.shape[1]), F32)
    for d in (3, 2, 1):
        incoming = chain(place[1] + d <= 3, after[d - 1], incoming, 0)
    return chain(place[2] == 0, other, incoming, 0)


def state_in(place, other, after):
    incoming = jnp.zeros((1, other.shape[1]), F32)
    for d in (3, 2, 1):
        incoming = chain(place[1] - d >= 0, after[3 - d], incoming, 2)
    return chain(place[2] == 1, other, incoming, 2)


def side_rows(core, turned, b):
    rows = turned.shape[0] // 4
    return turned[pl.ds(pl.multiple_of((2 * b + core) * rows, rows), rows), :]


def shares(core, turned, d, share, share_out, sems):
    step = 512
    saves = []
    rows = share.shape[0] // 2
    for i in range(d.shape[1] // step):
        part = slice(i * step, (i + 1) * step)
        for b in range(2):
            share[b * rows : (b + 1) * rows, part] = mxu(
                side_rows(core, turned, b), d[:, part]
            ).astype(BF16)
        saves.append(whole_copy(share.at[:, part], share_out.at[:, part], sems.at[i]))
        saves[i].start()
    return saves


def adjoint_kernel(
    place, outs, mix_ref, keep_ref, other, next1, next2, next3, local, turned,
    d_values, tails, share_out, share, s_sems,
):
    heads = local.shape[1] // LANES
    blocks = local.shape[0] // SPAN
    incoming = adjoint_in(place, other, (next1, next2, next3))

    def block(step, after):
        n = blocks - 1 - step
        rows = span(n)
        mix, keep = mix_ref[rows, :], keep_ref[rows, :]
        last = keep[SPAN - 1 : SPAN, :]
        fade = jnp.exp(last - keep)
        reach = jnp.exp(after)
        back = outs[pl.ds(n, 1), :]
        ends = []
        for h in range(heads):
            cols = head_cols(h)
            tail = back[:, cols] + reach[:, h : h + 1] * incoming[:, cols]
            ends.append(tail)
            full = local[rows, cols] + fade[:, h : h + 1] * tail
            d_values[rows, cols] = (mix[:, h : h + 1] * full).astype(BF16)
        tails[pl.ds(n, 1), :] = jnp.concatenate(ends, 1)
        return after + last

    lax.fori_loop(0, blocks, block, jnp.zeros((1, LANES), F32))
    saves = shares(1 - place[0] % 2, turned, d_values, share, share_out, s_sems)
    for c in saves:
        c.wait()


def router_kernel(
    place, ins, tails, keep_ref, stats_ref, decay, other, next1, next2, next3,
    local, values, adjoint, queries, keys,
    d_query, d_prev, dechunked_out, dechunked, d_sems,
):
    heads = values.shape[1] // LANES
    blocks = values.shape[0] // SPAN
    incoming = state_in(place, other, (next1, next2, next3))

    def block(n, before):
        rows = span(n)
        keep = keep_ref[rows, :]
        fade = jnp.exp(keep)
        last = keep[SPAN - 1 : SPAN, :]
        fade_back = jnp.exp(last - keep)
        reach = jnp.exp(before)
        start = ins[pl.ds(n, 1), :]
        tail = tails[pl.ds(n, 1), :]
        top = ids((SPAN, LANES), 0) == 0
        total = jnp.zeros((SPAN, LANES), F32)
        for h in range(heads):
            cols = head_cols(h)
            base = start[:, cols] + reach[:, h : h + 1] * incoming[:, cols]
            state = local[rows, cols] + fade[:, h : h + 1] * base
            dechunked[rows, cols] = state.astype(BF16)
            earlier = jnp.where(top, base, pltpu.roll(state, 1, 0))
            full = adjoint[rows, cols] + fade_back[:, h : h + 1] * tail[:, cols]
            total = total + (decay[:, h : h + 1] * full) * (values[rows, cols] - earlier)
        stats = stats_ref[rows, :]
        iq, ik, cosine, active = (stats[:, i : i + 1] for i in range(4))
        d_cos = -0.5 * (active * jnp.sum(total, -1, keepdims=True))
        both = d_cos * (iq * ik)
        over_q, over_k = d_cos * (cosine * iq * iq), d_cos * (cosine * ik * ik)
        q, k = queries[rows, :], keys[rows, :]
        d_query[rows, :] = (k * both - over_q * q).astype(BF16)
        d_prev[rows, :] = (q * both - over_k * k).astype(BF16)
        block_copy(dechunked, dechunked_out, d_sems, n).start()
        return before + last

    lax.fori_loop(0, blocks, block, jnp.zeros((1, LANES), F32))
    for n in range(blocks):
        block_copy(dechunked, dechunked_out, d_sems, n).wait()


def share_kernel(place, turned, d, share):
    step = 512
    rows = share.shape[0] // 2
    for i in range(d.shape[1] // step):
        part = slice(i * step, (i + 1) * step)
        for b in range(2):
            share[b * rows : (b + 1) * rows, part] = mxu(
                side_rows(1 - place[0] % 2, turned, b), d[:, part]
            ).astype(BF16)


def up_sum_kernel(place, d_values, theirs, turned, out):
    add_share(place, turned, d_values, theirs, out, out.shape[1] - d_values.shape[1])


def route_sum_kernel(place, d, theirs, partial, turned, out, *, at):
    add_share(place, turned, d, theirs, out, at)


def add_share(place, turned, d, theirs, out, at):
    step = 512
    rows = theirs.shape[0] // 2
    for i in range(d.shape[1] // step):
        part = slice(i * step, (i + 1) * step)
        for b in range(2):
            half = slice(b * rows, (b + 1) * rows)
            mine = mxu(side_rows(place[0] % 2, turned, b), d[:, part])
            total = mine + theirs[half, part].astype(F32)
            out[half, at + i * step : at + (i + 1) * step] = total.astype(BF16)


def tokens_kernel(place, d_query_in, d_key_in, d_values_in, *refs):
    pieces, out = refs[:16], refs[16]
    d_query, d_key, d_values, wq, wk, wu, d_sems, q_sems, k_sems, u_sems = refs[17:]
    loads = [
        whole_copy(source, target, d_sems.at[i])
        for i, (source, target) in enumerate(
            ((d_query_in, d_query), (d_key_in, d_key), (d_values_in, d_values))
        )
    ]
    for side in range(2):
        two, four = slice(2 * side, 2 * side + 2), slice(4 * side, 4 * side + 4)
        loads += fetch_panel(place, pieces[:4][two], wq.at[side], q_sems.at[side])
        loads += fetch_panel(place, pieces[4:8][two], wk.at[side], k_sems.at[side])
        loads += fetch_panel(place, pieces[8:][four], wu.at[side], u_sems.at[side])
    for c in loads:
        c.start()
    for c in loads:
        c.wait()
    dims = (((1,), (1,)), ((), ()))
    for side in range(2):
        index = side + (1 - 2 * side) * (place[0] // 2)
        terms = [
            lax.dot_general(d[...], w[side], dims, preferred_element_type=F32)
            for d, w in ((d_query, wq), (d_key, wk), (d_values, wu))
        ]
        out[:, panel_columns(index, wq.shape[1])] = (terms[0] + terms[1] + terms[2]).astype(BF16)


def sum_kernel(parts, out):
    step = 512
    for i in range(out.shape[2] // step):
        cols = slice(i * step, (i + 1) * step)
        acc = parts[0, :, cols].astype(F32)
        for j in range(1, parts.shape[0]):
            acc = acc + parts[j, :, cols].astype(F32)
        rounded = acc.astype(BF16)
        for j in range(out.shape[0]):
            out[j, :, cols] = rounded


def sum_ranks(exchanged, copies):
    _, depth, width = exchanged.shape
    return pl.pallas_call(
        sum_kernel,
        out_shape=jax.ShapeDtypeStruct((copies, depth, width), BF16),
        in_specs=[VMEM],
        out_specs=VMEM,
        compiler_params=pltpu.CompilerParams(vmem_limit_bytes=16 << 20),
    )(exchanged)


def widen_kernel(parts, *refs):
    outs, bufs, sems = refs[:3], refs[3:6], refs[6]
    ranks, depth, _ = parts.shape
    chunks = 4
    group = ranks // chunks
    copies = []
    for i in range(chunks):
        start = 0
        for o, (out, buf) in enumerate(zip(outs, bufs)):
            width = out.shape[1]
            for j in range(i * group, (i + 1) * group):
                buf[j * depth : (j + 1) * depth, :] = parts[j, :, start : start + width].astype(F32)
            rows = pl.ds(i * group * depth, group * depth)
            copies.append(
                pltpu.make_async_copy(buf.at[rows, :], out.at[rows, :], sems.at[o * chunks + i])
            )
            copies[-1].start()
            start += width
    for c in copies:
        c.wait()


def widen(summed, widths):
    ranks, depth, _ = summed.shape
    shapes = [(ranks * depth, w) for w in widths]
    return pl.pallas_call(
        widen_kernel,
        out_shape=[jax.ShapeDtypeStruct(s, F32) for s in shapes],
        in_specs=[VMEM],
        out_specs=[HBM] * len(widths),
        scratch_shapes=[pltpu.VMEM(s, F32) for s in shapes] + [DMA((12,))],
        compiler_params=pltpu.CompilerParams(vmem_limit_bytes=16 << 20),
    )(summed)


SMEM = pl.BlockSpec(memory_space=pltpu.SMEM)
VMEM = pl.BlockSpec(memory_space=pltpu.VMEM)
HBM = pl.BlockSpec(memory_space=pltpu.HBM)
DMA = pltpu.SemaphoreType.DMA


def in_hbm(a):
    return pltpu.with_memory_space_constraint(a, pltpu.HBM)


def call(
    body, place, vmem_args, hbm_args, vmem_outs, hbm_outs, scratch, flops, limit, aliases=None
):
    return pl.pallas_call(
        body,
        out_shape=[jax.ShapeDtypeStruct(s, t) for s, t in vmem_outs]
        + [pltpu.HBM(s, t) for s, t in hbm_outs],
        in_specs=[SMEM] + [VMEM] * len(vmem_args) + [HBM] * len(hbm_args),
        out_specs=[VMEM] * len(vmem_outs) + [HBM] * len(hbm_outs),
        scratch_shapes=scratch,
        input_output_aliases=aliases or {},
        cost_estimate=pl.CostEstimate(flops=flops, bytes_accessed=1 << 20, transcendentals=0),
        compiler_params=pltpu.CompilerParams(vmem_limit_bytes=limit << 20),
    )(place, *vmem_args, *[in_hbm(a) for a in hbm_args])


def local_step(tokens, bounds, decay_rates, w_query, w_key, w_up, grad_out):
    _, length, width = tokens.shape
    hidden = w_up.shape[1]
    heads = decay_rates.shape[0]
    rows = w_query.shape[0]
    blocks = length // SPAN
    tok, cot = tokens[0], grad_out[0]
    core, high = lax.axis_index("core"), lax.axis_index("xh")
    place = jnp.stack(
        [lax.axis_index("xl") * 2 + core, lax.axis_index("z"), high]
    ).astype(jnp.int32)

    half = rows // 2
    up = (w_up[:half], w_up[half:])
    q2, k2 = along_x(w_query, -1), along_x(w_key, 1)
    q1, k1 = swap_core(w_query), swap_core(w_key)
    before = along_ctx(tok[-1:], 1)
    u2_low = along_x(up[0], -1)
    u2_high = along_x(up[1], 1)
    tok_prev = jnp.concatenate([before, tok[:-1]], 0)

    decay = jnp.pad(decay_rates, (0, LANES - heads))[None]
    ready, decay, place = lax.optimization_barrier((tok, decay, place))
    flat, wide, narrow = (length, width), (length, hidden), (length, LANES)
    square, tall, per_block = (2 * rows, width), (2 * rows, hidden), (blocks, hidden)
    buf = pltpu.VMEM
    q_part, turned = call(
        near_kernel, place, (ready,), (w_query, q1),
        ((flat, F32), ((width, length), BF16)), (),
        [buf(square, BF16), DMA((2,))], 1_000_000_000, 12,
    )
    q_part, up_low, up_high, q2, k2 = lax.optimization_barrier((q_part, *up, q2, k2))
    q3, k3 = swap_core(q2), swap_core(k2)
    u1 = (swap_core(up_low), swap_core(up_high))
    v_part, turned_prev = call(
        near_values_kernel, place, (tok, tok_prev), (*up, *u1),
        ((wide, F32), ((width, length), BF16)), (),
        [buf(tall, BF16), DMA((4,))], 2_000_000_000, 12,
    )
    queries, keys, local_adjoint, mix, keep, stats, outs, b_carry = call(
        rates_kernel, place,
        (bounds, decay, tok, tok_prev, cot, q_part),
        (q2, q3, w_key, k1, k2, k3),
        ((flat, F32), (flat, F32), (wide, F32), (narrow, F32), (narrow, F32), (narrow, F32),
         (per_block, F32), ((2, hidden), F32)),
        (),
        [buf(square, BF16), buf((width, width), BF16), DMA((2,)), DMA((2, 2))],
        6_000_000_000, 16,
    )
    u2_low, u2_high, keep_late = lax.optimization_barrier((u2_low, u2_high, keep))
    u3 = (swap_core(u2_low), swap_core(u2_high))
    values, local_states, ins, message = call(
        states_kernel, place,
        (mix, keep_late, tok, b_carry, v_part),
        (u2_low, u2_high, *u3),
        ((wide, F32), (wide, F32), (per_block, F32), ((3, hidden), F32)),
        (),
        [buf(tall, BF16), buf((1, hidden), F32), DMA((4,))],
        6_000_000_000, 16,
    )
    other = lax.ppermute(message, "xh", [(0, 1), (1, 0)])
    (pair,) = call(
        pair_kernel, place, (message, other), (), (((3, hidden), F32),), (), [], 1_000_000, 4
    )
    messages = [other] + [
        lax.ppermute(pair, "z", [(i, (i - d) % 4) for i in range(4)]) for d in (1, 2, 3)
    ]

    half_flat, half_wide = (2 * rows, width), (2 * rows, hidden)
    d_values, tails, up_share = call(
        adjoint_kernel, place,
        (outs, mix, keep, *messages, local_adjoint, turned),
        (),
        ((wide, BF16), (per_block, F32)),
        ((half_wide, BF16),),
        [buf(half_wide, BF16), DMA((4,))],
        3_000_000_000, 16,
    )
    up_theirs = swap_core(up_share)
    d_query, d_prev, dechunked = call(
        router_kernel, place,
        (ins, tails, keep, stats, decay, *messages, local_states, values, local_adjoint,
         queries, keys),
        (),
        ((flat, BF16), (flat, BF16)),
        ((wide, BF16),),
        [buf(wide, BF16), DMA((blocks,))],
        3_000_000_000, 16,
    )
    after = along_ctx(d_prev[:1], -1)
    (q_share,) = call(
        share_kernel, place, (turned, d_query), (), ((half_flat, BF16),), (), [], 500_000_000, 6
    )
    q_theirs = swap_core(q_share)
    d_prev_late, q_share = lax.optimization_barrier((d_prev, q_share))
    (k_share,) = call(
        share_kernel, place, (turned_prev, d_prev_late), (), ((half_flat, BF16),), (), [],
        500_000_000, 6,
    )
    k_theirs = swap_core(k_share)
    full = (2 * rows, 2 * width + hidden)
    (partial,) = call(
        up_sum_kernel, place,
        (d_values, up_theirs, turned), (), ((full, BF16),), (), [], 1_500_000_000, 8,
    )
    sums = partial
    for d, theirs, lhs, at in (
        (d_query, q_theirs, turned, 0), (d_prev, k_theirs, turned_prev, width)
    ):
        (sums,) = call(
            functools.partial(route_sum_kernel, at=at), place,
            (d, theirs, sums, lhs), (), ((full, BF16),), (), [], 700_000_000, 8, {3: 0},
        )
    pair_sum = sums
    exchanged = lax.all_to_all(
        pair_sum.reshape(64, -1, pair_sum.shape[1]), ("xl", "dp", "z", "xh"), 0, 0, tiled=True
    )
    summed = lax.all_to_all(sum_ranks(exchanged, 32), ("dp", "z", "xh"), 0, 0, tiled=True)

    d_key = jnp.concatenate([d_prev[1:], after], 0)
    (grad_tokens,) = call(
        tokens_kernel, place,
        (),
        (d_query, d_key, d_values, w_query, q1, q2, q3, w_key, k1, k2, k3,
         *up, *u1, u2_low, u2_high, *u3),
        ((flat, BF16),),
        (),
        [buf(flat, BF16), buf(flat, BF16), buf(wide, BF16), buf((2, *square), BF16),
         buf((2, *square), BF16), buf((2, *tall), BF16), DMA((3,)), DMA((2, 2)), DMA((2, 2)),
         DMA((2, 4))],
        5_000_000_000, 60,
    )
    grads = widen(summed, (width, width, hidden))
    return (dechunked[None], grad_tokens[None], *grads)


def solution(mesh):
    split = jax.sharding.Mesh(
        mesh.devices.reshape(4, 2, 2, 4, 2), ("dp", "xl", "core", "z", "xh")
    )
    rows = P(("xl", "core"), None)
    data = P(("dp", "xl", "core"), CTX, None)
    return jax.shard_map(
        local_step,
        mesh=split,
        in_specs=(data, P(("dp", "xl", "core"), CTX), P(), rows, rows, rows, data),
        out_specs=(data, data, rows, rows, rows),
        check_vma=False,
    )
```

```python
import functools

import jax
import jax.numpy as jnp
from jax import lax
from jax.experimental import pallas as pl
from jax.experimental.pallas import tpu as pltpu
from jax.sharding import PartitionSpec as P


SPAN = 128
LANES = 128
epsilon = 1e-06
CTX = ("z", "xh")
RANGES = 8
HIGHEST = lax.Precision.HIGHEST
F32 = jnp.float32
BF16 = jnp.bfloat16


def along_x(a, by):
    pairs = []
    for xl in range(2):
        for xh in range(2):
            x = (xh * 2 + xl + by) % 4
            pairs.append((xl * 2 + xh, (x % 2) * 2 + x // 2))
    return lax.ppermute(a, ("xl", "xh"), pairs)


def swap_core(a):
    return lax.ppermute(a, "core", [(0, 1), (1, 0)])


def along_ctx(a, by):
    return lax.ppermute(
        a, CTX, [(i, i + by) for i in range(RANGES) if 0 <= i + by < RANGES]
    )


def mxu(a, b):
    return jnp.dot(a, b, preferred_element_type=F32)


def halves(a):
    high = a.astype(BF16)
    return high, (a - high.astype(F32)).astype(BF16)


def ids(shape, dim):
    return lax.broadcasted_iota(jnp.int32, shape, dim)


def head_cols(h):
    return slice(h * LANES, (h + 1) * LANES)


def span(n):
    return pl.ds(pl.multiple_of(n * SPAN, SPAN), SPAN)


def fetch_panel(place, pieces, whole, sems):
    core = place[0] % 2
    split = len(pieces) // 2
    rows = whole.shape[0] // 2
    copies = []
    for j, piece in enumerate(pieces):
        part = piece.shape[0]
        start = (core ^ (j // split)) * rows + (j % split) * part
        copies.append(
            pltpu.make_async_copy(
                piece, whole.at[pl.ds(pl.multiple_of(start, part), part), :], sems.at[j]
            )
        )
    return copies


def block_copy(source, target, sems, n):
    return pltpu.make_async_copy(source.at[span(n), :], target.at[span(n), :], sems.at[n])


def whole_copy(source, target, sem):
    return pltpu.make_async_copy(source, target, sem)


def panel_columns(index, depth):
    return pl.ds(pl.multiple_of(index * depth, depth), depth)


def turn(core, tok, turned):
    rows = tok.shape[1] // 4
    for b in range(2):
        for c in range(2):
            start = pl.multiple_of((core ^ c) * 2 * rows + b * rows, rows)
            first = (2 * b + c) * rows
            turned[pl.ds(start, rows), :] = tok[:, first : first + rows].T


def near_kernel(place, tok, q0, q1, queries, turned, wq, q_sems):
    loads = fetch_panel(place, (q0, q1), wq, q_sems)
    for c in loads:
        c.start()
    turn(place[0] % 2, tok, turned)
    for c in loads:
        c.wait()
    queries[...] = mxu(tok[:, panel_columns(place[0] // 2, wq.shape[0])], wq[...])


def near_values_kernel(
    place, tok, tok_prev, u0, u1, u2, u3, values, turned_prev, wu, sems
):
    loads = fetch_panel(place, (u0, u1, u2, u3), wu, sems)
    for c in loads:
        c.start()
    turn(place[0] % 2, tok_prev, turned_prev)
    for c in loads:
        c.wait()
    values[...] = mxu(tok[:, panel_columns(place[0] // 2, wu.shape[0])], wu[...])


def rates_kernel(
    place, bounds, decay, tok, tok_prev, cot, q_part, q2, q3, k0, k1, k2, k3,
    queries, keys, adjoint, mix_out, keep_out, stats_out, outs, carry,
    wq, wk, q_sems, k_sems,
):
    hidden = adjoint.shape[1]
    heads = hidden // LANES
    blocks = adjoint.shape[0] // SPAN
    load_q = fetch_panel(place, (q2, q3), wq, q_sems)
    side, depth = place[0] // 2, wq.shape[0]
    load_k = []
    for i, pieces in enumerate(((k0, k1), (k2, k3))):
        rows = panel_columns(side + i * (1 - 2 * side), depth)
        load_k += fetch_panel(place, pieces, wk.at[rows, :], k_sems.at[i])
    for c in load_q + load_k:
        c.start()
    carry[0:1, :] = jnp.zeros((1, hidden), F32)
    carry[1:2, :] = jnp.ones((1, hidden), F32)
    cols = panel_columns(1 - side, depth)
    for c in load_q:
        c.wait()
    queries[...] = q_part[...] + mxu(tok[:, cols], wq[...])
    for c in load_k:
        c.wait()
    keys[...] = mxu(tok_prev[...], wk[...])

    @pl.loop(0, blocks)
    def _(step):
        n = blocks - 1 - step
        rows = span(n)
        q, k = queries[rows, :], keys[rows, :]
        iq = lax.rsqrt(jnp.sum(q * q, -1, keepdims=True) + epsilon)
        ik = lax.rsqrt(jnp.sum(k * k, -1, keepdims=True) + epsilon)
        cosine = jnp.sum(q * k, -1, keepdims=True) * iq * ik
        lane = ids((SPAN, LANES), 1)
        sub = ids((SPAN, LANES), 0)
        first = jnp.logical_and(place[1] + place[2] == 0, n == 0)
        opening = jnp.logical_and(first, ids((SPAN, 1), 0) == 0)
        prob = jnp.where(opening, 1.0, 0.5 * (1.0 - cosine))
        marks = jnp.broadcast_to(bounds[:, rows].astype(F32), (SPAN, SPAN)).T[:, 0:1]
        marked = jnp.where(opening, 1.0, marks)
        mix = (marked * prob) * decay[...]
        logs = jnp.log(1.0 - mix)
        lower = (sub >= lane).astype(F32)
        keep = jnp.dot(lower, logs, precision=HIGHEST, preferred_element_type=F32)
        keep_rows = keep.T
        active = jnp.where(opening, 0.0, marked)
        stats = jnp.where(
            lane == 0, iq, jnp.where(lane == 1, ik, jnp.where(lane == 2, cosine, active))
        )
        mix_out[rows, :] = mix
        keep_out[rows, :] = keep
        stats_out[rows, :] = stats
        outs[pl.ds(n, 1), :] = carry[0:1, :]
        total = jnp.exp(keep[SPAN - 1 : SPAN, :])
        mask = jnp.where(sub <= lane, 0.0, -1e30)
        for h in range(heads):
            cols = head_cols(h)
            gap = keep_rows[h : h + 1, :] - keep[:, h : h + 1]
            band = jnp.exp(gap + mask)
            local = mxu(band.astype(BF16), cot[rows, cols])
            adjoint[rows, cols] = local
            d = total[:, h : h + 1]
            carry[0:1, cols] = d * carry[0:1, cols] + (1.0 - mix[0:1, h : h + 1]) * local[0:1, :]
            carry[1:2, cols] = d * carry[1:2, cols]


def states_kernel(
    place, mix_ref, keep_ref, tok, b_carry, v_part, u4, u5, u6, u7,
    values, states, ins, message,
    wu, carry, u_sems,
):
    hidden = values.shape[1]
    heads = hidden // LANES
    blocks = values.shape[0] // SPAN
    loads = fetch_panel(place, (u4, u5, u6, u7), wu, u_sems)
    for c in loads:
        c.start()
    carry[...] = jnp.zeros_like(carry)
    message[0:2, :] = b_carry[...]
    cols = panel_columns(1 - place[0] // 2, wu.shape[0])
    for c in loads:
        c.wait()
    values[...] = v_part[...] + mxu(tok[:, cols], wu[...])

    @pl.loop(0, blocks)
    def _(n):
        rows = span(n)
        mix, keep = mix_ref[rows, :], keep_ref[rows, :]
        keep_rows = keep.T
        mask = jnp.where(ids((SPAN, LANES), 0) >= ids((SPAN, LANES), 1), 0.0, -1e30)
        ins[pl.ds(n, 1), :] = carry[0:1, :]
        total = jnp.exp(keep[SPAN - 1 : SPAN, :])
        for h in range(heads):
            cols = head_cols(h)
            gap = keep[:, h : h + 1] - keep_rows[h : h + 1, :]
            band = jnp.exp(gap + mask)
            band = band.astype(BF16)
            added, rest = halves(mix[:, h : h + 1] * values[rows, cols])
            local = mxu(band, added) + mxu(band, rest)
            states[rows, cols] = local
            carry[0:1, cols] = total[:, h : h + 1] * carry[0:1, cols] + local[SPAN - 1 : SPAN, :]

    message[2:3, :] = carry[...]


def chain(own, message, incoming, row):
    return jnp.where(own, message[1:2, :] * incoming + message[row : row + 1, :], incoming)


def pair_kernel(place, message, other, pair):
    low = jnp.where(place[2] == 0, message[...], other[...])
    high = jnp.where(place[2] == 0, other[...], message[...])
    pair[0:1, :] = low[1:2] * high[0:1] + low[0:1]
    pair[1:2, :] = low[1:2] * high[1:2]
    pair[2:3, :] = high[1:2] * low[2:3] + high[2:3]


def adjoint_in(place, other, after):
    incoming = jnp.zeros((1, other.shape[1]), F32)
    for d in (3, 2, 1):
        incoming = chain(place[1] + d <= 3, after[d - 1], incoming, 0)
    return chain(place[2] == 0, other, incoming, 0)


def state_in(place, other, after):
    incoming = jnp.zeros((1, other.shape[1]), F32)
    for d in (3, 2, 1):
        incoming = chain(place[1] - d >= 0, after[3 - d], incoming, 2)
    return chain(place[2] == 1, other, incoming, 2)


def shares(turned, d, share, share_out, sems):
    step = 512
    saves = []
    rows = share.shape[0]
    for i in range(d.shape[1] // step):
        part = slice(i * step, (i + 1) * step)
        share[:, part] = mxu(turned[rows:, :], d[:, part]).astype(BF16)
        saves.append(whole_copy(share.at[:, part], share_out.at[:, part], sems.at[i]))
        saves[i].start()
    return saves


def adjoint_kernel(
    place, outs, mix_ref, keep_ref, other, next1, next2, next3, local, turned,
    d_values, tails, share_out, share, s_sems,
):
    heads = local.shape[1] // LANES
    blocks = local.shape[0] // SPAN
    incoming = adjoint_in(place, other, (next1, next2, next3))

    def block(step, after):
        n = blocks - 1 - step
        rows = span(n)
        mix, keep = mix_ref[rows, :], keep_ref[rows, :]
        last = keep[SPAN - 1 : SPAN, :]
        fade = jnp.exp(last - keep)
        reach = jnp.exp(after)
        back = outs[pl.ds(n, 1), :]
        ends = []
        for h in range(heads):
            cols = head_cols(h)
            tail = back[:, cols] + reach[:, h : h + 1] * incoming[:, cols]
            ends.append(tail)
            full = local[rows, cols] + fade[:, h : h + 1] * tail
            d_values[rows, cols] = (mix[:, h : h + 1] * full).astype(BF16)
        tails[pl.ds(n, 1), :] = jnp.concatenate(ends, 1)
        return after + last

    lax.fori_loop(0, blocks, block, jnp.zeros((1, LANES), F32))
    saves = shares(turned, d_values, share, share_out, s_sems)
    for c in saves:
        c.wait()


def router_kernel(
    place, ins, tails, keep_ref, stats_ref, decay, other, next1, next2, next3,
    local, values, adjoint, queries, keys,
    d_query, d_prev, dechunked_out, dechunked, d_sems,
):
    heads = values.shape[1] // LANES
    blocks = values.shape[0] // SPAN
    incoming = state_in(place, other, (next1, next2, next3))

    def block(n, before):
        rows = span(n)
        keep = keep_ref[rows, :]
        fade = jnp.exp(keep)
        last = keep[SPAN - 1 : SPAN, :]
        fade_back = jnp.exp(last - keep)
        reach = jnp.exp(before)
        start = ins[pl.ds(n, 1), :]
        tail = tails[pl.ds(n, 1), :]
        top = ids((SPAN, LANES), 0) == 0
        total = jnp.zeros((SPAN, LANES), F32)
        for h in range(heads):
            cols = head_cols(h)
            base = start[:, cols] + reach[:, h : h + 1] * incoming[:, cols]
            state = local[rows, cols] + fade[:, h : h + 1] * base
            dechunked[rows, cols] = state.astype(BF16)
            earlier = jnp.where(top, base, pltpu.roll(state, 1, 0))
            full = adjoint[rows, cols] + fade_back[:, h : h + 1] * tail[:, cols]
            total = total + (decay[:, h : h + 1] * full) * (values[rows, cols] - earlier)
        stats = stats_ref[rows, :]
        iq, ik, cosine, active = (stats[:, i : i + 1] for i in range(4))
        d_cos = -0.5 * (active * jnp.sum(total, -1, keepdims=True))
        both = d_cos * (iq * ik)
        over_q, over_k = d_cos * (cosine * iq * iq), d_cos * (cosine * ik * ik)
        q, k = queries[rows, :], keys[rows, :]
        d_query[rows, :] = (k * both - over_q * q).astype(BF16)
        d_prev[rows, :] = (q * both - over_k * k).astype(BF16)
        block_copy(dechunked, dechunked_out, d_sems, n).start()
        return before + last

    lax.fori_loop(0, blocks, block, jnp.zeros((1, LANES), F32))
    for n in range(blocks):
        block_copy(dechunked, dechunked_out, d_sems, n).wait()


def share_kernel(turned, d, share):
    step = 512
    rows = share.shape[0]
    for i in range(d.shape[1] // step):
        part = slice(i * step, (i + 1) * step)
        share[:, part] = mxu(turned[rows:, :], d[:, part]).astype(BF16)


def sum_share_kernel(d, theirs, turned, *refs, at):
    out = refs[-1]
    step = 512
    rows = theirs.shape[0]
    for i in range(d.shape[1] // step):
        part = slice(i * step, (i + 1) * step)
        total = mxu(turned[0:rows, :], d[:, part]) + theirs[:, part].astype(F32)
        out[:, at + i * step : at + (i + 1) * step] = total.astype(BF16)


def tokens_kernel(place, d_query_in, d_key_in, d_values_in, *refs):
    pieces, out = refs[:16], refs[16]
    d_query, d_key, d_values, wq, wk, wu, d_sems, q_sems, k_sems, u_sems = refs[17:]
    loads = [
        whole_copy(source, target, d_sems.at[i])
        for i, (source, target) in enumerate(
            ((d_query_in, d_query), (d_key_in, d_key), (d_values_in, d_values))
        )
    ]
    for side in range(2):
        two, four = slice(2 * side, 2 * side + 2), slice(4 * side, 4 * side + 4)
        loads += fetch_panel(place, pieces[:4][two], wq.at[side], q_sems.at[side])
        loads += fetch_panel(place, pieces[4:8][two], wk.at[side], k_sems.at[side])
        loads += fetch_panel(place, pieces[8:][four], wu.at[side], u_sems.at[side])
    for c in loads:
        c.start()
    for c in loads:
        c.wait()
    dims = (((1,), (1,)), ((), ()))
    for side in range(2):
        index = side + (1 - 2 * side) * (place[0] // 2)
        terms = [
            lax.dot_general(d[...], w[side], dims, preferred_element_type=F32)
            for d, w in ((d_query, wq), (d_key, wk), (d_values, wu))
        ]
        out[:, panel_columns(index, wq.shape[1])] = (terms[0] + terms[1] + terms[2]).astype(BF16)


def sum_kernel(parts, out):
    step = 512
    for i in range(out.shape[2] // step):
        cols = slice(i * step, (i + 1) * step)
        acc = parts[0, :, cols].astype(F32)
        for j in range(1, parts.shape[0]):
            acc = acc + parts[j, :, cols].astype(F32)
        rounded = acc.astype(BF16)
        for j in range(out.shape[0]):
            out[j, :, cols] = rounded


def sum_ranks(exchanged, copies):
    _, depth, width = exchanged.shape
    return pl.pallas_call(
        sum_kernel,
        out_shape=jax.ShapeDtypeStruct((copies, depth, width), BF16),
        in_specs=[VMEM],
        out_specs=VMEM,
        compiler_params=pltpu.CompilerParams(vmem_limit_bytes=16 << 20),
    )(exchanged)


def widen_kernel(parts, *refs):
    outs, bufs, sems = refs[:3], refs[3:6], refs[6]
    ranks, depth, _ = parts.shape
    chunks = 4
    group = ranks // chunks
    copies = []
    for i in range(chunks):
        start = 0
        for o, (out, buf) in enumerate(zip(outs, bufs)):
            width = out.shape[1]
            for j in range(i * group, (i + 1) * group):
                buf[j * depth : (j + 1) * depth, :] = parts[j, :, start : start + width].astype(F32)
            rows = pl.ds(i * group * depth, group * depth)
            copies.append(
                pltpu.make_async_copy(buf.at[rows, :], out.at[rows, :], sems.at[o * chunks + i])
            )
            copies[-1].start()
            start += width
    for c in copies:
        c.wait()


def widen(summed, widths):
    ranks, depth, _ = summed.shape
    shapes = [(ranks * depth, w) for w in widths]
    return pl.pallas_call(
        widen_kernel,
        out_shape=[jax.ShapeDtypeStruct(s, F32) for s in shapes],
        in_specs=[VMEM],
        out_specs=[HBM] * len(widths),
        scratch_shapes=[pltpu.VMEM(s, F32) for s in shapes] + [DMA((12,))],
        compiler_params=pltpu.CompilerParams(vmem_limit_bytes=16 << 20),
    )(summed)


SMEM = pl.BlockSpec(memory_space=pltpu.SMEM)
VMEM = pl.BlockSpec(memory_space=pltpu.VMEM)
HBM = pl.BlockSpec(memory_space=pltpu.HBM)
DMA = pltpu.SemaphoreType.DMA


def call(
    body, place, vmem_args, hbm_args, vmem_outs, hbm_outs, scratch, flops, limit, aliases=None
):
    return pl.pallas_call(
        body,
        out_shape=[jax.ShapeDtypeStruct(s, t) for s, t in vmem_outs]
        + [pltpu.HBM(s, t) for s, t in hbm_outs],
        in_specs=([] if place is None else [SMEM])
        + [VMEM] * len(vmem_args)
        + [HBM] * len(hbm_args),
        out_specs=[VMEM] * len(vmem_outs) + [HBM] * len(hbm_outs),
        scratch_shapes=scratch,
        input_output_aliases=aliases or {},
        cost_estimate=pl.CostEstimate(flops=flops, bytes_accessed=1 << 20, transcendentals=0),
        compiler_params=pltpu.CompilerParams(vmem_limit_bytes=limit << 20),
    )(*(() if place is None else (place,)), *vmem_args, *hbm_args)


def local_step(tokens, bounds, decay_rates, w_query, w_key, w_up, grad_out):
    _, length, width = tokens.shape
    hidden = w_up.shape[1]
    heads = decay_rates.shape[0]
    rows = w_query.shape[0]
    blocks = length // SPAN
    tok, cot = tokens[0], grad_out[0]
    core, high = lax.axis_index("core"), lax.axis_index("xh")
    place = jnp.stack(
        [lax.axis_index("xl") * 2 + core, lax.axis_index("z"), high]
    ).astype(jnp.int32)

    half = rows // 2
    up = (w_up[:half], w_up[half:])
    q2, k2 = along_x(w_query, -1), along_x(w_key, 1)
    q1, k1 = swap_core(w_query), swap_core(w_key)
    before = along_ctx(tok[-1:], 1)
    u2_low = along_x(up[0], -1)
    u2_high = along_x(up[1], 1)
    tok_prev = jnp.concatenate([before, tok[:-1]], 0)

    decay = jnp.pad(decay_rates, (0, LANES - heads))[None]
    ready, decay, place = lax.optimization_barrier((tok, decay, place))
    flat, wide, narrow = (length, width), (length, hidden), (length, LANES)
    square, tall, per_block = (2 * rows, width), (2 * rows, hidden), (blocks, hidden)
    buf = pltpu.VMEM
    q_part, turned = call(
        near_kernel, place, (ready,), (w_query, q1),
        ((flat, F32), ((width, length), BF16)), (),
        [buf(square, BF16), DMA((2,))], 1_000_000_000, 12,
    )
    q_part, up_low, up_high, q2, k2 = lax.optimization_barrier((q_part, *up, q2, k2))
    q3, k3 = swap_core(q2), swap_core(k2)
    u1 = (swap_core(up_low), swap_core(up_high))
    v_part, turned_prev = call(
        near_values_kernel, place, (tok, tok_prev), (*up, *u1),
        ((wide, F32), ((width, length), BF16)), (),
        [buf(tall, BF16), DMA((4,))], 2_000_000_000, 12,
    )
    queries, keys, local_adjoint, mix, keep, stats, outs, b_carry = call(
        rates_kernel, place,
        (bounds, decay, tok, tok_prev, cot, q_part),
        (q2, q3, w_key, k1, k2, k3),
        ((flat, F32), (flat, F32), (wide, F32), (narrow, F32), (narrow, F32), (narrow, F32),
         (per_block, F32), ((2, hidden), F32)),
        (),
        [buf(square, BF16), buf((width, width), BF16), DMA((2,)), DMA((2, 2))],
        6_000_000_000, 16,
    )
    u2_low, u2_high, keep_late = lax.optimization_barrier((u2_low, u2_high, keep))
    u3 = (swap_core(u2_low), swap_core(u2_high))
    values, local_states, ins, message = call(
        states_kernel, place,
        (mix, keep_late, tok, b_carry, v_part),
        (u2_low, u2_high, *u3),
        ((wide, F32), (wide, F32), (per_block, F32), ((3, hidden), F32)),
        (),
        [buf(tall, BF16), buf((1, hidden), F32), DMA((4,))],
        6_000_000_000, 16,
    )
    other = lax.ppermute(message, "xh", [(0, 1), (1, 0)])
    (pair,) = call(
        pair_kernel, place, (message, other), (), (((3, hidden), F32),), (), [], 1_000_000, 4
    )
    messages = [other] + [
        lax.ppermute(pair, "z", [(i, (i - d) % 4) for i in range(4)]) for d in (1, 2, 3)
    ]

    half_flat, half_wide = (2 * rows, width), (2 * rows, hidden)
    d_values, tails, up_share = call(
        adjoint_kernel, place,
        (outs, mix, keep, *messages, local_adjoint, turned),
        (),
        ((wide, BF16), (per_block, F32)),
        ((half_wide, BF16),),
        [buf(half_wide, BF16), DMA((4,))],
        3_000_000_000, 16,
    )
    up_theirs = swap_core(up_share)
    d_query, d_prev, dechunked = call(
        router_kernel, place,
        (ins, tails, keep, stats, decay, *messages, local_states, values, local_adjoint,
         queries, keys),
        (),
        ((flat, BF16), (flat, BF16)),
        ((wide, BF16),),
        [buf(wide, BF16), DMA((blocks,))],
        3_000_000_000, 16,
    )
    after = along_ctx(d_prev[:1], -1)
    (q_share,) = call(
        share_kernel, None, (turned, d_query), (), ((half_flat, BF16),), (), [], 500_000_000, 6
    )
    q_theirs = swap_core(q_share)
    d_prev_late, q_share = lax.optimization_barrier((d_prev, q_share))
    (k_share,) = call(
        share_kernel, None, (turned_prev, d_prev_late), (), ((half_flat, BF16),), (), [],
        500_000_000, 6,
    )
    k_theirs = swap_core(k_share)
    full = (2 * rows, 2 * width + hidden)
    sums = ()
    for d, theirs, lhs, at in (
        (d_values, up_theirs, turned, 2 * width),
        (d_query, q_theirs, turned, 0),
        (d_prev, k_theirs, turned_prev, width),
    ):
        sums = call(
            functools.partial(sum_share_kernel, at=at), None,
            (d, theirs, lhs, *sums), (), ((full, BF16),), (), [], 700_000_000, 8,
            {3: 0} if sums else None,
        )
    (pair_sum,) = sums
    exchanged = lax.all_to_all(
        pair_sum.reshape(64, -1, pair_sum.shape[1]), ("xl", "dp", "z", "xh"), 0, 0, tiled=True
    )
    summed = lax.all_to_all(sum_ranks(exchanged, 32), ("dp", "z", "xh"), 0, 0, tiled=True)

    d_key = jnp.concatenate([d_prev[1:], after], 0)
    (grad_tokens,) = call(
        tokens_kernel, place,
        (),
        (d_query, d_key, d_values, w_query, q1, q2, q3, w_key, k1, k2, k3,
         *up, *u1, u2_low, u2_high, *u3),
        ((flat, BF16),),
        (),
        [buf(flat, BF16), buf(flat, BF16), buf(wide, BF16), buf((2, *square), BF16),
         buf((2, *square), BF16), buf((2, *tall), BF16), DMA((3,)), DMA((2, 2)), DMA((2, 2)),
         DMA((2, 4))],
        5_000_000_000, 60,
    )
    grads = widen(summed, (width, width, hidden))
    return (dechunked[None], grad_tokens[None], *grads)


def solution(mesh):
    split = jax.sharding.Mesh(
        mesh.devices.reshape(4, 2, 2, 4, 2), ("dp", "xl", "core", "z", "xh")
    )
    rows = P(("xl", "core"), None)
    data = P(("dp", "xl", "core"), CTX, None)
    return jax.shard_map(
        local_step,
        mesh=split,
        in_specs=(data, P(("dp", "xl", "core"), CTX), P(), rows, rows, rows, data),
        out_specs=(data, data, rows, rows, rows),
        check_vma=False,
    )
```
